32 devices in a mesh: rep: 8 (over z, y), fsdp: 4 (over x, core).
Axes of the slice: x: 2, y: 2, z: 4, core: 2. Of those that a mesh axis runs over, the one named last changes fastest.
Arguments:
- block_input: bfloat16 [8, 1024, 576], P('rep', 'fsdp'), may hold values from -45 to 45, as said below
- query_weight: bfloat16 [576, 576], P('fsdp'), as said below
- key_weight: bfloat16 [576, 192], P('fsdp'), as said below
- value_weight: bfloat16 [576, 192], P('fsdp'), may hold values from -0.25 to 0.25
- out_weight: bfloat16 [576, 576], P('fsdp'), may hold values from -1 to 1
- gate_weight: bfloat16 [576, 1536], P('fsdp'), may hold values from -0.25 to 0.25
- up_weight: bfloat16 [576, 1536], P('fsdp'), may hold values from -0.25 to 0.25
- down_weight: bfloat16 [1536, 576], P('fsdp'), may hold values from -0.15625 to 0.15625
- attn_gain: bfloat16 [576], P('fsdp'), may hold values from 0.099609375 to 1.8984375
- mlp_gain: bfloat16 [576], P('fsdp'), may hold values from 0.099609375 to 1.8984375
- segment_ids: int32 [8, 1024], P('rep'), may hold values from 0 to 7, as said below
- doc_positions: int32 [8, 1024], P('rep', 'fsdp'), may hold values from 0 to 1023, as said below
- out_cotangent: bfloat16 [8, 1024, 576], P('rep', 'fsdp'), may hold values from -6 to 6
Outputs:
- block_output: bfloat16 [8, 1024, 576], P('rep', 'fsdp')
- grad_input: bfloat16 [8, 1024, 576], P('rep', 'fsdp')
- grad_query_weight: float32 [576, 576], P('fsdp')
- grad_key_weight: float32 [576, 192], P('fsdp')
- grad_value_weight: float32 [576, 192], P('fsdp')
- grad_out_weight: float32 [576, 576], P('fsdp')
- grad_gate_weight: float32 [576, 1536], P('fsdp')
- grad_up_weight: float32 [576, 1536], P('fsdp')
- grad_down_weight: float32 [1536, 576], P('fsdp')
- grad_attn_gain: float32 [576], P('fsdp')
- grad_mlp_gain: float32 [576], P('fsdp')
The draws below stay inside these ranges and needn't reach their ends.
Inputs may be any that keep to these rules, and one draw needn't show every extreme that they name: `segment_ids`: segment numbers never fall along a sequence; a document is the run of tokens with one number, and holds at least 65 tokens. `doc_positions`: the position of each token within its document of segment_ids, counting from 0 at the document's first token. `block_input`: finite values. `query_weight`: finite values. `key_weight`: finite values.
All inputs are finite; a program needn't handle non-finite values.
Results may differ from the reference program's by a relative error of at most 0.017.
Values may be sent and summed in bfloat16 or wider, within the bound.
No kernel may reach another device: no remote copies, remote signals or barrier semaphores. Data moves between devices by JAX's collectives and lax.ppermute only.
A program may use at most 128 MiB of HBM per device.

```python
import math
import jax
import jax.numpy as jnp
from jax import lax

D = 576
FF = 1536
QH = 9
KVH = 3
HD = 64
SEQ_LEN = 1024
SEQUENCES = 8
QW = 576
KW = 192


def draw_block_input(key, part):
    lowest = math.log(0.3)
    highest = math.log(3.0)
    row_scale = jnp.exp(jax.random.uniform(jax.random.fold_in(key, 1), (SEQUENCES, SEQ_LEN, 1), minval=lowest, maxval=highest))
    col_scale = jnp.exp(jax.random.uniform(jax.random.fold_in(key, 2), (D,), minval=lowest, maxval=highest))
    noise = jnp.clip(jax.random.normal(jax.random.fold_in(key, 3), (SEQUENCES, SEQ_LEN, D)), -5.0, 5.0)
    return (noise * row_scale * col_scale).astype(jnp.bfloat16)


def draw_key_weight(key, part):
    basis = jnp.clip(jax.random.normal(jax.random.fold_in(key, 12), (D, KVH, HD)), -5.0, 5.0) / math.sqrt(D)
    return basis.reshape(D, KVH * HD).astype(jnp.bfloat16)


def draw_query_weight(key, part):
    group_size = QH // KVH
    own_part = jnp.clip(jax.random.normal(jax.random.fold_in(key, 13), (D, KVH, group_size, HD)), -5.0, 5.0) / math.sqrt(D)
    return own_part.reshape(D, QH * HD).astype(jnp.bfloat16)


def doc_layout(key):
    grid_step = SEQ_LEN // 8
    offsets = jax.random.randint(jax.random.fold_in(key, 21), (SEQUENCES, 7), 0, grid_step // 2)
    kept_bounds = jax.random.randint(jax.random.fold_in(key, 22), (SEQUENCES, 7), 0, 2)
    seq_index = jnp.arange(SEQUENCES, dtype=jnp.int32)[:, None]
    kept_bounds = jnp.where(seq_index == SEQUENCES - 1, 0, kept_bounds)
    kept_bounds = jnp.where(seq_index == 0, 1, kept_bounds)
    bounds = jnp.arange(1, 8, dtype=jnp.int32)[None, :] * grid_step + offsets
    token_index = jnp.arange(SEQ_LEN, dtype=jnp.int32)[None, :, None]
    active = (kept_bounds[:, None, :] == 1) & (token_index >= bounds[:, None, :])
    numbers = jnp.max(jnp.where(active, jnp.arange(1, 8, dtype=jnp.int32)[None, None, :], 0), axis=-1)
    starts = jnp.max(jnp.where(active, bounds[:, None, :], 0), axis=-1)
    positions = jnp.arange(SEQ_LEN, dtype=jnp.int32)[None, :] - starts
    return (numbers.astype(jnp.int32), positions.astype(jnp.int32))


def draw_segment_ids(key, part):
    return doc_layout(key)[0]


def draw_doc_positions(key, part):
    return doc_layout(key)[1]


def steps_of(own_key, shape, pieces, least, largest):
    level, own = 1.0, jax.random.fold_in(own_key, 6)
    for axis_at, blocks in pieces:
        heights = jnp.exp(jax.random.uniform(jax.random.fold_in(own, axis_at), (blocks,), jnp.float32, least / len(pieces), largest / len(pieces)))
        level = level * jnp.repeat(heights, shape[axis_at] // blocks).reshape([-1 if axis == axis_at else 1 for axis in range(len(shape))])
    return level


def centred(stream_key, extent, spread, reach, shards=(), kind=jnp.bfloat16):
    result = jax.random.normal(stream_key, extent, jnp.float32) * spread
    if len(shards) > 0:
        result = steps_of(stream_key, extent, shards, -0.22, 0.18) * result
    return jnp.clip(result, min=-reach, max=reach).astype(kind)


def setup_inputs(seed: int = 0) -> dict:
    key_of = jax.random.split(jax.random.key(seed), 14)
    return {
        "block_input": draw_block_input(jax.random.fold_in(key_of[13], 71), 0),
        "query_weight": draw_query_weight(jax.random.fold_in(key_of[13], 71), 0),
        "key_weight": draw_key_weight(jax.random.fold_in(key_of[13], 71), 0),
        "value_weight": centred(key_of[3], (D, KW), D ** -0.5, 0.25, ((0, 4),)),
        "out_weight": centred(key_of[4], (QW, D), (QW // 16) ** -0.5, 1.0, ((0, 4),)),
        "gate_weight": centred(key_of[5], (D, FF), D ** -0.5, 0.25, ((0, 4),)),
        "up_weight": centred(key_of[6], (D, FF), D ** -0.5, 0.25, ((0, 4),)),
        "down_weight": centred(key_of[7], (FF, D), FF ** -0.5, 0.15625, ((0, 4),)),
        "attn_gain": jnp.clip(1.0 + 0.18 * jax.random.normal(key_of[8], (D,), jnp.float32), 0.099609375, 1.8984375).astype(jnp.bfloat16),
        "mlp_gain": jnp.clip(1.0 + 0.18 * jax.random.normal(key_of[9], (D,), jnp.float32), 0.099609375, 1.8984375).astype(jnp.bfloat16),
        "segment_ids": draw_segment_ids(jax.random.fold_in(key_of[13], 71), 0),
        "doc_positions": draw_doc_positions(jax.random.fold_in(key_of[13], 71), 0),
        "out_cotangent": centred(key_of[12], (SEQUENCES, SEQ_LEN, D), 1.0, 6.0, ((0, 8), (1, 4))),
    }


EPS = 1e-05
THETA = 100000.0

def rms_forward(stream, gain_vector):
    inverse_rms = lax.rsqrt(lax.optimization_barrier(jnp.mean(stream * stream, axis=-1, keepdims=True)) + EPS)
    return (stream * inverse_rms * gain_vector, inverse_rms)

def rms_backward(stream, inverse_rms, gain_vector, grad_norm):
    scaled = grad_norm * gain_vector
    grad_gain = lax.optimization_barrier(jnp.sum(grad_norm * stream * inverse_rms, axis=0))
    cubed = inverse_rms * inverse_rms * inverse_rms
    grad_stream = inverse_rms * scaled - stream * cubed * lax.optimization_barrier(jnp.mean(scaled * stream, axis=-1, keepdims=True))
    return (grad_stream, grad_gain)

def rope_tables(positions):
    inverse_freq = 1.0 / THETA ** (jnp.arange(0, HD, 2).astype(jnp.float32) / HD)
    angles = positions.astype(jnp.float32)[:, None] * inverse_freq[None, :]
    angles = jnp.concatenate([angles, angles], axis=-1)
    return (jnp.cos(angles)[:, None, :], jnp.sin(angles)[:, None, :])

def rotate_half(values):
    half_width = values.shape[-1] // 2
    return jnp.concatenate([-values[..., half_width:], values[..., :half_width]], axis=-1)

def rotate(values, cosines, sines, rotation_sign):
    return values * cosines + rotation_sign * rotate_half(values) * sines

def masked_scores(query_rows, key_rows, key_mask):
    scores = jnp.einsum('qkgd,tkd->kgqt', query_rows.astype(jnp.float32), key_rows.astype(jnp.float32))
    scores = scores * (1.0 / math.sqrt(HD))
    return jnp.where(key_mask[None, None], scores, -1e+30)

def attend(query_rows, key_rows, value_rows, key_mask):
    scores = masked_scores(query_rows, key_rows, key_mask)
    row_max = lax.optimization_barrier(jnp.max(scores, axis=-1, keepdims=True))
    log_total = row_max + jnp.log(lax.optimization_barrier(jnp.sum(jnp.exp(scores - row_max), axis=-1, keepdims=True)))
    attn_probs = jnp.where(key_mask[None, None], jnp.exp(scores - log_total), 0.0)
    probs_low = lax.optimization_barrier(attn_probs.astype(jnp.bfloat16))
    context = jnp.einsum('kgqt,tkd->qkgd', probs_low.astype(jnp.float32), value_rows.astype(jnp.float32))
    return (context.astype(jnp.bfloat16), log_total)

def attend_back(query_rows, key_rows, value_rows, key_mask, log_total, grad_context):
    scores = masked_scores(query_rows, key_rows, key_mask)
    attn_probs = jnp.where(key_mask[None, None], jnp.exp(scores - log_total), 0.0)
    probs_low = lax.optimization_barrier(attn_probs.astype(jnp.bfloat16))
    grad_ctx32 = grad_context.astype(jnp.float32)
    grad_values = jnp.einsum('kgqt,qkgd->tkd', probs_low.astype(jnp.float32), grad_ctx32)
    grad_probs = jnp.einsum('qkgd,tkd->kgqt', grad_ctx32, value_rows.astype(jnp.float32))
    dot_total = lax.optimization_barrier(jnp.sum(attn_probs * grad_probs, axis=-1, keepdims=True))
    grad_scores = attn_probs * (grad_probs - dot_total) * (1.0 / math.sqrt(HD))
    scores_low = lax.optimization_barrier(grad_scores.astype(jnp.bfloat16)).astype(jnp.float32)
    grad_queries = jnp.einsum('kgqt,tkd->qkgd', scores_low, key_rows.astype(jnp.float32))
    grad_keys = jnp.einsum('kgqt,qkgd->tkd', scores_low, query_rows.astype(jnp.float32))
    return (grad_queries, grad_keys, grad_values)

def block_pass(inputs_low, cotangent_low, seq_segs, seq_positions, weights):
    query_weight, key_weight, value_weight, out_weight, gate_weight, up_weight, down_weight, attn_gain, mlp_gain = weights
    seq_length = inputs_low.shape[0]
    group_size = QH // KVH
    inputs = inputs_low.astype(jnp.float32)
    gain_first = attn_gain.astype(jnp.float32)
    gain_second = mlp_gain.astype(jnp.float32)
    norm_first, inverse_first = rms_forward(inputs, gain_first)
    normed_first = norm_first.astype(jnp.bfloat16)
    query_proj = jnp.dot(normed_first, query_weight, preferred_element_type=jnp.float32)
    key_proj = jnp.dot(normed_first, key_weight, preferred_element_type=jnp.float32)
    value_proj = jnp.dot(normed_first, value_weight, preferred_element_type=jnp.float32)
    cosines, sines = rope_tables(seq_positions)
    query_rows = rotate(query_proj.reshape(seq_length, QH, HD), cosines, sines, 1.0).astype(jnp.bfloat16)
    query_rows = query_rows.reshape(seq_length, KVH, group_size, HD)
    key_rows = rotate(key_proj.reshape(seq_length, KVH, HD), cosines, sines, 1.0).astype(jnp.bfloat16)
    value_rows = value_proj.astype(jnp.bfloat16).reshape(seq_length, KVH, HD)
    token_index = jnp.arange(seq_length, dtype=jnp.int32)
    key_mask = (seq_segs[:, None] == seq_segs[None, :]) & (token_index[None, :] <= token_index[:, None])
    context, log_total = attend(query_rows, key_rows, value_rows, key_mask)
    context_rows = context.reshape(seq_length, QH * HD)
    stream = inputs + jnp.dot(context_rows, out_weight, preferred_element_type=jnp.float32)
    norm_second, inverse_second = rms_forward(stream, gain_second)
    normed_second = norm_second.astype(jnp.bfloat16)
    gate_proj = jnp.dot(normed_second, gate_weight, preferred_element_type=jnp.float32)
    up_proj = jnp.dot(normed_second, up_weight, preferred_element_type=jnp.float32)
    activation = (jax.nn.silu(gate_proj) * up_proj).astype(jnp.bfloat16)
    outputs = (stream + jnp.dot(activation, down_weight, preferred_element_type=jnp.float32)).astype(jnp.bfloat16)
    grad_outputs = cotangent_low.astype(jnp.float32)
    grad_down = jnp.dot(activation.T, cotangent_low, preferred_element_type=jnp.float32)
    grad_act = jnp.dot(cotangent_low, down_weight.T, preferred_element_type=jnp.float32)
    sigma = jax.nn.sigmoid(gate_proj)
    grad_gate_pre = (grad_act * up_proj * sigma * (1.0 + gate_proj * (1.0 - sigma))).astype(jnp.bfloat16)
    grad_up_pre = (grad_act * gate_proj * sigma).astype(jnp.bfloat16)
    grad_gate = jnp.dot(normed_second.T, grad_gate_pre, preferred_element_type=jnp.float32)
    grad_up = jnp.dot(normed_second.T, grad_up_pre, preferred_element_type=jnp.float32)
    grad_norm_second = jnp.dot(grad_gate_pre, gate_weight.T, preferred_element_type=jnp.float32)
    grad_norm_second = grad_norm_second + jnp.dot(grad_up_pre, up_weight.T, preferred_element_type=jnp.float32)
    grad_stream_norm, grad_mlp_gain = rms_backward(stream, inverse_second, gain_second, grad_norm_second)
    grad_stream = grad_outputs + grad_stream_norm
    grad_stream_low = grad_stream.astype(jnp.bfloat16)
    grad_out = jnp.dot(context_rows.T, grad_stream_low, preferred_element_type=jnp.float32)
    grad_context = jnp.dot(grad_stream_low, out_weight.T, preferred_element_type=jnp.float32).astype(jnp.bfloat16)
    grad_context = grad_context.reshape(seq_length, KVH, group_size, HD)
    grad_queries, grad_keys, grad_values = attend_back(query_rows, key_rows, value_rows, key_mask, log_total, grad_context)
    grad_query_pre = rotate(grad_queries.reshape(seq_length, QH, HD), cosines, sines, -1.0).astype(jnp.bfloat16)
    grad_query_pre = grad_query_pre.reshape(seq_length, QH * HD)
    grad_key_pre = rotate(grad_keys, cosines, sines, -1.0).astype(jnp.bfloat16).reshape(seq_length, KVH * HD)
    grad_value_pre = grad_values.astype(jnp.bfloat16).reshape(seq_length, KVH * HD)
    grad_query = jnp.dot(normed_first.T, grad_query_pre, preferred_element_type=jnp.float32)
    grad_key = jnp.dot(normed_first.T, grad_key_pre, preferred_element_type=jnp.float32)
    grad_value = jnp.dot(normed_first.T, grad_value_pre, preferred_element_type=jnp.float32)
    grad_norm_first = jnp.dot(grad_query_pre, query_weight.T, preferred_element_type=jnp.float32)
    grad_norm_first = grad_norm_first + jnp.dot(grad_key_pre, key_weight.T, preferred_element_type=jnp.float32)
    grad_norm_first = grad_norm_first + jnp.dot(grad_value_pre, value_weight.T, preferred_element_type=jnp.float32)
    grad_input_norm, grad_attn_gain = rms_backward(inputs, inverse_first, gain_first, grad_norm_first)
    grad_inputs = (grad_stream + grad_input_norm).astype(jnp.bfloat16)
    grads = (grad_query, grad_key, grad_value, grad_out, grad_gate, grad_up, grad_down, grad_attn_gain, grad_mlp_gain)
    return (outputs, grad_inputs, grads)

def reference(block_input, query_weight, key_weight, value_weight, out_weight, gate_weight, up_weight, down_weight, attn_gain, mlp_gain, segment_ids, doc_positions, out_cotangent):
    weights = (query_weight, key_weight, value_weight, out_weight, gate_weight, up_weight, down_weight, attn_gain, mlp_gain)
    start_totals = tuple((jnp.zeros(weight.shape, jnp.float32) for weight in weights))

    def scan_step(totals, slices):
        inputs_seq, cotangent_seq, segs_seq, positions_seq = slices
        outputs, grad_inputs, grads = block_pass(inputs_seq, cotangent_seq, segs_seq, positions_seq, weights)
        totals = tuple((running + added for running, added in zip(totals, grads)))
        return (totals, (outputs, grad_inputs))
    totals, stacked = lax.scan(scan_step, start_totals, (block_input, out_cotangent, segment_ids, doc_positions))
    return (stacked[0], stacked[1], totals[0], totals[1], totals[2], totals[3], totals[4], totals[5], totals[6], totals[7], totals[8])
```

```python
import math

import jax
import jax.numpy as jnp
from jax import lax
from jax.sharding import PartitionSpec as P

QH = 9
KVH = 3
HD = 64


EPS = 1e-05
THETA = 100000.0


def rms_forward(stream, gain_vector):
    inverse_rms = lax.rsqrt(jnp.mean(stream * stream, axis=-1, keepdims=True) + EPS)
    return (stream * inverse_rms * gain_vector, inverse_rms)


def rms_backward(stream, inverse_rms, gain_vector, grad_norm):
    scaled = grad_norm * gain_vector
    grad_gain = jnp.sum(grad_norm * stream * inverse_rms, axis=0)
    cubed = inverse_rms * inverse_rms * inverse_rms
    grad_stream = inverse_rms * scaled - stream * cubed * jnp.mean(
        scaled * stream, axis=-1, keepdims=True
    )
    return (grad_stream, grad_gain)


def rope_tables(positions):
    inverse_freq = 1.0 / THETA ** (jnp.arange(0, HD, 2).astype(jnp.float32) / HD)
    angles = positions.astype(jnp.float32)[:, None] * inverse_freq[None, :]
    angles = jnp.concatenate([angles, angles], axis=-1)
    return (jnp.cos(angles)[:, None, :], jnp.sin(angles)[:, None, :])


def rotate_half(values):
    half_width = values.shape[-1] // 2
    return jnp.concatenate([-values[..., half_width:], values[..., :half_width]], axis=-1)


def rotate(values, cosines, sines, rotation_sign):
    return values * cosines + rotation_sign * rotate_half(values) * sines


def masked_scores(query_rows, key_rows, key_mask):
    scores = jnp.einsum("qkgd,tkd->kgqt", query_rows, key_rows, preferred_element_type=jnp.float32)
    scores = scores * (1.0 / math.sqrt(HD))
    return jnp.where(key_mask[None, None], scores, -1e30)


def attend(query_rows, key_rows, value_rows, key_mask):
    scores = masked_scores(query_rows, key_rows, key_mask)
    row_max = jnp.max(scores, axis=-1, keepdims=True)
    log_total = row_max + jnp.log(jnp.sum(jnp.exp(scores - row_max), axis=-1, keepdims=True))
    attn_probs = jnp.where(key_mask[None, None], jnp.exp(scores - log_total), 0.0).astype(
        jnp.bfloat16
    )
    context = jnp.einsum(
        "kgqt,tkd->qkgd", attn_probs, value_rows, preferred_element_type=jnp.float32
    )
    return (context.astype(jnp.bfloat16), log_total)


def attend_back(query_rows, key_rows, value_rows, key_mask, log_total, grad_context):
    scores = masked_scores(query_rows, key_rows, key_mask)
    attn_probs = jnp.where(key_mask[None, None], jnp.exp(scores - log_total), 0.0)
    probs_low = attn_probs.astype(jnp.bfloat16)
    grad_values = jnp.einsum(
        "kgqt,qkgd->tkd", probs_low, grad_context, preferred_element_type=jnp.float32
    )
    grad_probs = jnp.einsum(
        "qkgd,tkd->kgqt", grad_context, value_rows, preferred_element_type=jnp.float32
    )
    dot_total = jnp.sum(attn_probs * grad_probs, axis=-1, keepdims=True)
    scores_low = (attn_probs * (grad_probs - dot_total) * (1.0 / math.sqrt(HD))).astype(
        jnp.bfloat16
    )
    grad_queries = jnp.einsum(
        "kgqt,tkd->qkgd", scores_low, key_rows, preferred_element_type=jnp.float32
    )
    grad_keys = jnp.einsum(
        "kgqt,qkgd->tkd", scores_low, query_rows, preferred_element_type=jnp.float32
    )
    return (grad_queries, grad_keys, grad_values)


def swap(values, axis, size, bit):
    return lax.ppermute(values, axis, [(i, i ^ (1 << bit)) for i in range(size)])


def bits_of(size):
    return size.bit_length() - 1


def gather(shard, size, me):
    held = [(0, shard)]
    for bit in reversed(range(bits_of(size))):
        held += [(r ^ (1 << bit), swap(block, "fsdp", size, bit)) for r, block in held]
    rows = shard.shape[0]
    whole = jnp.zeros((size * rows,) + shard.shape[1:], shard.dtype)
    for r, block in held:
        whole = lax.dynamic_update_slice_in_dim(whole, block, (me ^ r) * rows, 0)
    return whole


def pick(values, index, axis):
    return lax.dynamic_index_in_dim(values, index, axis, keepdims=False)


def scatter_sum(parts, size, me):
    rows = parts.shape[0] // size
    parts = parts.reshape((size, rows) + parts.shape[1:])
    for bit in range(bits_of(size)):
        mine = (me >> bit) & 1
        pairs = parts.reshape((parts.shape[0] // 2, 2) + parts.shape[1:])
        arrived = swap(pick(pairs, 1 - mine, 1), "fsdp", size, bit)
        parts = pick(pairs, mine, 1) + arrived
    return parts.reshape((rows,) + parts.shape[2:])


def total_over(shard, size, me, axis, unit):
    steps = []
    for bit in range(bits_of(size)):
        length = shard.shape[axis]
        mine = (me >> bit) & 1
        halved = length % (2 * unit) == 0
        steps.append((bit, mine, halved))
        if halved:
            half = length // 2
            sent = lax.dynamic_slice_in_dim(shard, (1 - mine) * half, half, axis)
            kept = lax.dynamic_slice_in_dim(shard, mine * half, half, axis)
            shard = kept + swap(sent, "rep", size, bit)
        else:
            shard = shard + swap(shard, "rep", size, bit)
    for bit, mine, halved in reversed(steps):
        if halved:
            other = swap(shard, "rep", size, bit)
            shard = jnp.where(
                mine == 0,
                jnp.concatenate([shard, other], axis),
                jnp.concatenate([other, shard], axis),
            )
    return shard.astype(jnp.float32)


def shards(
    fsdp,
    rep,
    block_input,
    query_weight,
    key_weight,
    value_weight,
    out_weight,
    gate_weight,
    up_weight,
    down_weight,
    attn_gain,
    mlp_gain,
    segment_ids,
    doc_positions,
    out_cotangent,
):
    num_seqs, local_rows, width = block_input.shape
    seq_length = segment_ids.shape[1]
    group_size = QH // KVH
    tokens = num_seqs * local_rows
    me = lax.axis_index("fsdp")
    me_rep = lax.axis_index("rep")
    low = jnp.bfloat16
    own = width // fsdp
    qw, kw, ff = query_weight.shape[1], key_weight.shape[1], gate_weight.shape[1]

    proj_own = jnp.concatenate([query_weight, key_weight, value_weight], 1)
    gain_rows = jnp.zeros((16, proj_own.shape[1]), low)
    gain_rows = gain_rows.at[0, :own].set(attn_gain).at[1, :own].set(mlp_gain)
    first = gather(jnp.concatenate([proj_own, gain_rows], 0), fsdp, me)
    first = first.reshape(fsdp, own + 16, qw + 2 * kw)
    proj_full = first[:, :own].reshape(width, qw + 2 * kw)
    gain_first = first[:, own, :own].reshape(width).astype(jnp.float32)
    gain_second = first[:, own + 1, :own].reshape(width).astype(jnp.float32)

    inputs = block_input.reshape(tokens, width).astype(jnp.float32)
    norm_first, inverse_first = rms_forward(inputs, gain_first)
    normed_first = norm_first.astype(low)
    proj = jnp.dot(normed_first, proj_full, preferred_element_type=jnp.float32)
    query_proj, key_proj, value_proj = proj[:, :qw], proj[:, qw : qw + kw], proj[:, qw + kw :]
    cosines, sines = rope_tables(doc_positions.reshape(tokens))
    query_rows = rotate(query_proj.reshape(tokens, QH, HD), cosines, sines, 1.0).astype(low)
    query_rows = query_rows.reshape(num_seqs, local_rows, KVH, group_size, HD)
    key_rows = rotate(key_proj.reshape(tokens, KVH, HD), cosines, sines, 1.0).astype(low)
    key_values = jnp.concatenate([key_rows.reshape(tokens, kw), value_proj.astype(low)], 1)
    key_values = key_values.reshape(num_seqs, local_rows, 2 * kw).transpose(1, 0, 2)
    all_kv = gather(key_values, fsdp, me).transpose(1, 0, 2)
    all_keys = all_kv[..., :kw].reshape(num_seqs, seq_length, KVH, HD)
    all_values = all_kv[..., kw:].reshape(num_seqs, seq_length, KVH, HD)

    out_full = gather(out_weight, fsdp, me)
    gate_up_full = gather(jnp.concatenate([gate_weight, up_weight], 1), fsdp, me)
    down_full = gather(down_weight, fsdp, me)

    query_segs = lax.dynamic_slice_in_dim(segment_ids, me * local_rows, local_rows, 1)
    query_index = me * local_rows + jnp.arange(local_rows, dtype=jnp.int32)
    key_index = jnp.arange(seq_length, dtype=jnp.int32)

    def make_mask(own_segs, seq_segs):
        return (own_segs[:, None] == seq_segs[None, :]) & (
            key_index[None, :] <= query_index[:, None]
        )

    def forward_one(slices):
        queries_seq, keys_seq, values_seq, own_segs, seq_segs = slices
        return attend(queries_seq, keys_seq, values_seq, make_mask(own_segs, seq_segs))

    context, log_total = lax.map(
        forward_one, (query_rows, all_keys, all_values, query_segs, segment_ids)
    )
    context_rows = context.reshape(tokens, QH * HD)
    stream = inputs + jnp.dot(context_rows, out_full, preferred_element_type=jnp.float32)
    norm_second, inverse_second = rms_forward(stream, gain_second)
    normed_second = norm_second.astype(low)
    gate_up = jnp.dot(normed_second, gate_up_full, preferred_element_type=jnp.float32)
    gate_proj, up_proj = gate_up[:, :ff], gate_up[:, ff:]
    sigma = jax.nn.sigmoid(gate_proj)
    activation = (gate_proj * sigma * up_proj).astype(low)
    outputs = (stream + jnp.dot(activation, down_full, preferred_element_type=jnp.float32)).astype(
        low
    )
    cotangent_low = out_cotangent.reshape(tokens, width)
    grad_outputs = cotangent_low.astype(jnp.float32)
    grad_down = jnp.dot(activation.T, cotangent_low, preferred_element_type=jnp.float32).astype(low)
    down_shard = scatter_sum(grad_down, fsdp, me)
    grad_act = jnp.dot(cotangent_low, down_full.T, preferred_element_type=jnp.float32)
    grad_gate_pre = (grad_act * up_proj * sigma * (1.0 + gate_proj * (1.0 - sigma))).astype(low)
    grad_up_pre = (grad_act * gate_proj * sigma).astype(low)
    grad_pre = jnp.concatenate([grad_gate_pre, grad_up_pre], 1)
    grad_gate_up = jnp.dot(normed_second.T, grad_pre, preferred_element_type=jnp.float32).astype(low)
    gate_up_shard = scatter_sum(grad_gate_up, fsdp, me)
    down_total = total_over(down_shard, rep, me_rep, 0, 16)
    gate_up_total = total_over(gate_up_shard, rep, me_rep, 1, 128)
    grad_norm_second = jnp.dot(grad_pre, gate_up_full.T, preferred_element_type=jnp.float32)
    grad_stream_norm, grad_mlp_gain = rms_backward(
        stream, inverse_second, gain_second, grad_norm_second
    )
    grad_stream = grad_outputs + grad_stream_norm
    grad_stream_low = grad_stream.astype(low)
    grad_out = jnp.dot(context_rows.T, grad_stream_low, preferred_element_type=jnp.float32).astype(
        low
    )
    grad_context = jnp.dot(grad_stream_low, out_full.T, preferred_element_type=jnp.float32).astype(
        low
    )
    grad_context = grad_context.reshape(num_seqs, local_rows, KVH, group_size, HD)

    def backward_one(slices):
        queries_seq, keys_seq, values_seq, own_segs, seq_segs, totals_seq, grad_seq = slices
        return attend_back(
            queries_seq, keys_seq, values_seq, make_mask(own_segs, seq_segs), totals_seq, grad_seq
        )

    grad_queries, grad_keys_part, grad_values_part = lax.map(
        backward_one,
        (query_rows, all_keys, all_values, query_segs, segment_ids, log_total, grad_context),
    )
    kv_part = jnp.concatenate(
        [
            grad_keys_part.reshape(num_seqs, seq_length, kw),
            grad_values_part.reshape(num_seqs, seq_length, kw),
        ],
        2,
    ).astype(low)
    kv_local = scatter_sum(kv_part.transpose(1, 0, 2), fsdp, me).transpose(1, 0, 2)
    kv_local = kv_local.reshape(tokens, 2 * kw)
    grad_keys_local = kv_local[:, :kw].astype(jnp.float32).reshape(tokens, KVH, HD)
    grad_query_pre = rotate(grad_queries.reshape(tokens, QH, HD), cosines, sines, -1.0).astype(low)
    grad_key_pre = rotate(grad_keys_local, cosines, sines, -1.0).astype(low)
    grad_proj_pre = jnp.concatenate(
        [
            grad_query_pre.reshape(tokens, qw),
            grad_key_pre.reshape(tokens, kw),
            kv_local[:, kw:],
        ],
        1,
    )
    grad_proj = jnp.dot(normed_first.T, grad_proj_pre, preferred_element_type=jnp.float32).astype(
        low
    )
    grad_norm_first = jnp.dot(grad_proj_pre, proj_full.T, preferred_element_type=jnp.float32)
    grad_input_norm, grad_attn_gain = rms_backward(
        inputs, inverse_first, gain_first, grad_norm_first
    )
    grad_inputs = (grad_stream + grad_input_norm).astype(low)
    gains = jnp.stack([grad_attn_gain, grad_mlp_gain]).astype(low).reshape(2, fsdp, own)
    gains = jnp.pad(gains.transpose(1, 0, 2), ((0, 0), (0, 14), (0, grad_proj.shape[1] - own)))
    last = jnp.concatenate([grad_proj.reshape(fsdp, own, qw + 2 * kw), gains], 1)
    last = jnp.concatenate(
        [
            last,
            jnp.pad(grad_out.reshape(fsdp, own, width), ((0, 0), (0, 16), (0, 0))),
        ],
        2,
    )
    last_shard = scatter_sum(last.reshape(fsdp * (own + 16), -1), fsdp, me)
    last_total = total_over(last_shard, rep, me_rep, 1, 128)
    edge = qw + 2 * kw
    return (
        outputs.reshape(num_seqs, local_rows, width),
        grad_inputs.reshape(num_seqs, local_rows, width),
        last_total[:own, :qw],
        last_total[:own, qw : qw + kw],
        last_total[:own, qw + kw : edge],
        last_total[:own, edge:],
        gate_up_total[:, :ff],
        gate_up_total[:, ff:],
        down_total,
        last_total[own, :own],
        last_total[own + 1, :own],
    )


def solution(mesh):
    in_specs = (
        P("rep", "fsdp", None),
        P("fsdp", None),
        P("fsdp", None),
        P("fsdp", None),
        P("fsdp", None),
        P("fsdp", None),
        P("fsdp", None),
        P("fsdp", None),
        P("fsdp"),
        P("fsdp"),
        P("rep", None),
        P("rep", "fsdp"),
        P("rep", "fsdp", None),
    )
    out_specs = (
        P("rep", "fsdp", None),
        P("rep", "fsdp", None),
        P("fsdp", None),
        P("fsdp", None),
        P("fsdp", None),
        P("fsdp", None),
        P("fsdp", None),
        P("fsdp", None),
        P("fsdp", None),
        P("fsdp"),
        P("fsdp"),
    )

    def body(*arrays):
        return shards(mesh.shape["fsdp"], mesh.shape["rep"], *arrays)

    return jax.shard_map(body, mesh=mesh, in_specs=in_specs, out_specs=out_specs, check_vma=False)
```

```python
import functools

import jax
import jax.numpy as jnp
from jax import lax
from jax.experimental import pallas as pl
from jax.experimental.pallas import tpu as pltpu
from jax.sharding import PartitionSpec as P


QH = 9
KVH = 3
HD = 64
GROUP = QH // KVH

EPS = 1e-05
THETA = 100000.0
LOW = jnp.bfloat16
F32 = jnp.float32
GAIN_ROWS = 16

VMEM = pl.BlockSpec(memory_space=pltpu.VMEM)
SMEM = pl.BlockSpec(memory_space=pltpu.SMEM)


def dot(a, b):
    return lax.dot_general(a, b, (((1,), (0,)), ((), ())), preferred_element_type=F32)


def dot_nt(a, b):
    return lax.dot_general(a, b, (((1,), (1,)), ((), ())), preferred_element_type=F32)


def dot_tn(a, b):
    return lax.dot_general(a, b, (((0,), (0,)), ((), ())), preferred_element_type=F32)


def call(body, outs, scratch, flops, nbytes, *operands):
    return pl.pallas_call(
        body,
        out_shape=[jax.ShapeDtypeStruct(s, d) for s, d in outs],
        in_specs=[SMEM] + [VMEM] * (len(operands) - 1),
        out_specs=[VMEM] * len(outs),
        scratch_shapes=[pltpu.VMEM(s, d) for s, d in scratch],
        cost_estimate=pl.CostEstimate(flops=flops, bytes_accessed=nbytes, transcendentals=0),
    )(*operands)


def inverse_root(stream):
    return lax.rsqrt(jnp.mean(stream * stream, axis=-1, keepdims=True) + EPS)


def norm_back(stream, gain, grad_norm):
    root = inverse_root(stream)
    scaled = grad_norm * gain
    grad_gain = jnp.sum(grad_norm * stream * root, axis=0, keepdims=True)
    inner = jnp.mean(scaled * stream, axis=-1, keepdims=True)
    return root * scaled - stream * (root * root * root) * inner, grad_gain


def turned(values, cosines, sines, sign):
    lane = lax.broadcasted_iota(jnp.int32, cosines.shape, 1) % HD
    parts = []
    for at in range(0, values.shape[1], 128):
        part = values[:, at : at + 128]
        half = jnp.where(lane < HD // 2, -pltpu.roll(part, 96, 1), pltpu.roll(part, 32, 1))
        parts.append(part * cosines + sign * half * sines)
    return jnp.concatenate(parts, 1) if len(parts) > 1 else parts[0]


def split_columns(values, target, count):
    width = values.shape[1] // count
    for j in range(count):
        target[j] = values[:, j * width : (j + 1) * width]


def join_columns(source, count):
    return jnp.concatenate([source[j] for j in range(count)], 1)


def project_body(fsdp, rel, table, xt_ref, cos_ref, sin_ref, *refs):
    weights, refs = refs[:fsdp], refs[fsdp:]
    n1_ref, q_ref, kv_ref, gain_ref, gain_sc, n1_sc, acc_sc = refs
    me = table[0]
    own = n1_ref.shape[1] // fsdp
    for r, w in zip(rel, weights):
        gain_sc[me ^ r] = w[own : own + GAIN_ROWS, :own].astype(F32)
    gains = join_columns(gain_sc, fsdp)
    gain_ref[...] = gains
    x = xt_ref[...].astype(F32).T
    n1 = (x * inverse_root(x) * gains[0:1]).astype(LOW)
    n1_ref[...] = n1
    split_columns(n1, n1_sc, fsdp)
    for i, (r, w) in enumerate(zip(rel, weights)):
        part = dot(n1_sc[me ^ r], w[:own, :])
        acc_sc[...] = part if i == 0 else acc_sc[...] + part
    qw = q_ref.shape[1]
    kw = kv_ref.shape[1] // 2
    qk = turned(acc_sc[:, : qw + kw], cos_ref[...], sin_ref[...], 1.0).astype(LOW)
    q_ref[...] = qk[:, :qw]
    kv_ref[...] = jnp.concatenate([qk[:, qw:], acc_sc[:, qw + kw :].astype(LOW)], 1)


def load_heads(rel, me, q_ref, kv_refs, q_sc, k_sc, v_sc):
    rows = q_ref.shape[0]
    for h in range(QH):
        q_sc[h] = q_ref[:, h * HD : (h + 1) * HD]
    for r, kv in zip(rel, kv_refs):
        at = pl.ds(pl.multiple_of((me ^ r) * rows, rows), rows)
        for h in range(KVH):
            k_sc[h, at, :] = kv[:, h * HD : (h + 1) * HD]
            v_sc[h, at, :] = kv[:, (KVH + h) * HD : (KVH + h + 1) * HD]


def fill_mask(me, rows, seg_ref, mask_sc):
    keys = mask_sc.shape[0]
    seg = seg_ref[...].astype(F32)
    key_seg = jnp.broadcast_to(seg, (8, keys)).T[:, 0:1]
    query_seg = seg_ref[:, pl.ds(pl.multiple_of(me * rows, rows), rows)].astype(F32)
    key = lax.broadcasted_iota(jnp.int32, (keys, rows), 0)
    query = lax.broadcasted_iota(jnp.int32, (keys, rows), 1) + me * rows
    allowed = (key_seg == query_seg) & (key <= query)
    mask_sc[...] = jnp.where(allowed, 0.0, -1e30)


def attend_body(fsdp, rel, table, q_ref, seg_ref, xt_ref, gain_ref, *refs):
    kv_refs, refs = refs[:fsdp], refs[fsdp:]
    out_refs, refs = refs[:fsdp], refs[fsdp:]
    ctx_ref, lse_ref, h1_ref, n2_ref, q_sc, k_sc, v_sc, mask_sc, ctx_t, ctx_sc = refs
    me = table[0]
    rows = q_ref.shape[0]
    load_heads(rel, me, q_ref, kv_refs, q_sc, k_sc, v_sc)
    fill_mask(me, rows, seg_ref, mask_sc)

    @pl.loop(0, KVH)
    def _(kh):
        keys = k_sc[kh]
        values_t = v_sc[kh].T
        for g in range(GROUP):
            h = kh * GROUP + g
            mask = mask_sc[...]
            s = jnp.where(mask < 0.0, mask, dot_nt(keys, q_sc[h]) * (HD**-0.5))
            top = jnp.max(s, axis=0, keepdims=True)
            e = jnp.exp(s - top)
            total = jnp.sum(e, axis=0, keepdims=True)
            lse_ref[h] = jnp.broadcast_to(top + jnp.log(total), (8, rows))
            p = (e * (1.0 / total)).astype(LOW)
            at = pl.ds(pl.multiple_of(h * HD, HD), HD)
            ctx_t[at, :] = dot(values_t, p)

    ctx = ctx_t[...].T.astype(LOW)
    ctx_ref[...] = ctx
    split_columns(ctx, ctx_sc, fsdp)
    h1 = xt_ref[...].astype(F32).T
    for r, w in zip(rel, out_refs):
        h1 = h1 + dot(ctx_sc[me ^ r], w[...])
    h1_ref[...] = h1
    n2_ref[...] = (h1 * inverse_root(h1) * gain_ref[1:2]).astype(LOW)


def feed_body(fsdp, rel, table, n2_ref, dyt_ref, *refs):
    gu_refs, refs = refs[:fsdp], refs[fsdp:]
    gp_ref, up_ref, act_ref, keep_ref, send_ref, n2_sc = refs
    me = table[0]
    ff = gp_ref.shape[1]
    split_columns(n2_ref[...], n2_sc, fsdp)
    chunk = ff // 4

    @pl.loop(0, 4)
    def _(c):
        left = pl.ds(pl.multiple_of(c * chunk, chunk), chunk)
        right = pl.ds(pl.multiple_of(ff + c * chunk, chunk), chunk)
        gp = up = None
        for r, w in zip(rel, gu_refs):
            n2 = n2_sc[me ^ r]
            g, u = dot(n2, w[:, left]), dot(n2, w[:, right])
            gp, up = (g, u) if gp is None else (gp + g, up + u)
        gp_ref[:, left] = gp
        up_ref[:, left] = up
        act_ref[:, left] = (gp * jax.nn.sigmoid(gp) * up).astype(LOW)

    rows = ff // fsdp
    for r in range(fsdp):
        at = pl.ds(pl.multiple_of((me ^ r) * rows, rows), rows)
        target = send_ref if r & 1 else keep_ref
        target[r // 2] = dot(dyt_ref[...], act_ref[:, at]).astype(LOW)


def feed_back_body(fsdp, rel, table, gp_ref, up_ref, act_ref, dyt_ref, h1_ref, n2_ref, *refs):
    down_refs, refs = refs[:fsdp], refs[fsdp:]
    yt_ref, dgu_ref, keep_ref, send_ref, n2_sc = refs
    me = table[0]
    ff = gp_ref.shape[1]
    split_columns(n2_ref[...], n2_sc, fsdp)
    rows = ff // fsdp
    y = h1_ref[...]
    dy = dyt_ref[...].T
    for r, w in zip(rel, down_refs):
        at = pl.ds(pl.multiple_of((me ^ r) * rows, rows), rows)
        right = pl.ds(pl.multiple_of(ff + (me ^ r) * rows, rows), rows)
        y = y + dot_nt(act_ref[:, at], w[...])
        da = dot(dy, w[...])
        gp, up = gp_ref[:, at], up_ref[:, at]
        sg = jax.nn.sigmoid(gp)
        dgu_ref[:, at] = (da * up * sg * (1.0 + gp * (1.0 - sg))).astype(LOW)
        dgu_ref[:, right] = (da * gp * sg).astype(LOW)
    yt_ref[...] = y.T.astype(LOW)
    chunk = ff // 2

    @pl.loop(0, 4)
    def _(c):
        at = pl.ds(pl.multiple_of(c * chunk, chunk), chunk)
        for r in range(fsdp):
            target = send_ref if r & 1 else keep_ref
            target[c // 2, r // 2, :, pl.ds(pl.multiple_of((c % 2) * chunk, chunk), chunk)] = (
                dot_tn(n2_sc[me ^ r], dgu_ref[:, at]).astype(LOW)
            )


def stream_back_body(fsdp, rel, table, dgu_ref, dyt_ref, h1_ref, gain_ref, ctx_ref, *refs):
    gu_refs, refs = refs[:fsdp], refs[fsdp:]
    out_refs, refs = refs[:fsdp], refs[fsdp:]
    dh1_ref, dctx_ref, keep_ref, send_ref, gain_out, dn_sc, ctx_sc, dctx_sc = refs
    me = table[0]
    for r, w in zip(rel, gu_refs):
        dn_sc[me ^ r] = dot_nt(dgu_ref[...], w[...])
    dv, grad_gain = norm_back(h1_ref[...], gain_ref[1:2], join_columns(dn_sc, fsdp))
    gain_out[...] = jnp.broadcast_to(grad_gain, gain_out.shape)
    dh1 = dyt_ref[...].astype(F32).T + dv
    dh1_ref[...] = dh1
    low = dh1.astype(LOW)
    for r, w in zip(rel, out_refs):
        dctx_sc[me ^ r] = dot_nt(low, w[...])
    dctx_ref[...] = join_columns(dctx_sc, fsdp).astype(LOW)
    split_columns(ctx_ref[...], ctx_sc, fsdp)
    for r in range(fsdp):
        target = send_ref if r & 1 else keep_ref
        target[r // 2] = dot_tn(ctx_sc[me ^ r], low).astype(LOW)


def attend_back_body(
    fsdp, rel, table, q_ref, seg_ref, lse_ref, dctx_ref, cos_ref, sin_ref, *refs
):
    kv_refs, refs = refs[:fsdp], refs[fsdp:]
    dqp_ref, keep_ref, send_ref = refs[:3]
    q_sc, k_sc, v_sc, mask_sc, dctx_sc, dq_t, dk_sc, dv_sc = refs[3:]
    me = table[0]
    rows = q_ref.shape[0]
    load_heads(rel, me, q_ref, kv_refs, q_sc, k_sc, v_sc)
    fill_mask(me, rows, seg_ref, mask_sc)
    for h in range(QH):
        dctx_sc[h] = dctx_ref[:, h * HD : (h + 1) * HD]

    @pl.loop(0, KVH)
    def _(kh):
        keys = k_sc[kh]
        values = v_sc[kh]
        keys_t = keys.T
        for g in range(GROUP):
            h = kh * GROUP + g
            mask = mask_sc[...]
            s = jnp.where(mask < 0.0, mask, dot_nt(keys, q_sc[h]) * (HD**-0.5))
            p = jnp.exp(s - lse_ref[h, 0:1, :])
            dv = dot(p.astype(LOW), dctx_sc[h])
            dp = dot_nt(values, dctx_sc[h])
            inner = jnp.sum(p * dp, axis=0, keepdims=True)
            ds = (p * (dp - inner) * (HD**-0.5)).astype(LOW)
            dk = dot(ds, q_sc[h])
            dk_sc[kh] = dk if g == 0 else dk_sc[kh] + dk
            dv_sc[kh] = dv if g == 0 else dv_sc[kh] + dv
            at = pl.ds(pl.multiple_of(h * HD, HD), HD)
            dq_t[at, :] = dot(keys_t, ds)

    extra = dq_t.shape[0] - QH * HD
    dq_t[QH * HD :, :] = jnp.zeros((extra, rows), F32)
    dq = turned(dq_t[...].T, cos_ref[...], sin_ref[...], -1.0)
    dqp_ref[...] = dq[:, : QH * HD].astype(LOW)
    for r in range(fsdp):
        at = pl.ds(pl.multiple_of((me ^ r) * rows, rows), rows)
        target = send_ref if r & 1 else keep_ref
        target[r // 2] = jnp.concatenate(
            [dk_sc[h, at, :] for h in range(KVH)] + [dv_sc[h, at, :] for h in range(KVH)], 1
        ).astype(LOW)


def project_back_body(
    fsdp, rel, table, xt_ref, n1_ref, dqp_ref, dkv_ref, dh1_ref, cos_ref, sin_ref, gain_ref,
    mlp_gain_ref, *refs
):
    weights, refs = refs[:fsdp], refs[fsdp:]
    dxt_ref, keep_ref, send_ref, n1_sc, dproj_sc, dn_sc, gain_sc = refs
    me = table[0]
    own = n1_ref.shape[1] // fsdp
    kw = dkv_ref.shape[1] // 2
    dkv = dkv_ref[...]
    dk = jnp.concatenate([dkv[:, :kw].astype(F32), jnp.zeros((dkv.shape[0], 256 - kw), F32)], 1)
    dkp = turned(dk, cos_ref[...], sin_ref[...], -1.0)[:, :kw].astype(LOW)
    dproj_sc[...] = jnp.concatenate([dqp_ref[...], dkp, dkv[:, kw:]], 1)
    for r, w in zip(rel, weights):
        dn_sc[me ^ r] = dot_nt(dproj_sc[...], w[:own, :])
    dv, grad_gain = norm_back(xt_ref[...].astype(F32).T, gain_ref[0:1], join_columns(dn_sc, fsdp))
    dxt_ref[...] = (dh1_ref[...] + dv).T.astype(LOW)
    gains = jnp.concatenate(
        [grad_gain, mlp_gain_ref[0:1], jnp.zeros((GAIN_ROWS - 2, grad_gain.shape[1]), F32)], 0
    ).astype(LOW)
    split_columns(gains, gain_sc, fsdp)
    split_columns(n1_ref[...], n1_sc, fsdp)
    for r in range(fsdp):
        target = send_ref if r & 1 else keep_ref
        target[r // 2, :own, :] = dot_tn(n1_sc[me ^ r], dproj_sc[...]).astype(LOW)
        target[r // 2, own:, :own] = gain_sc[me ^ r]
        target[r // 2, own:, own:] = jnp.zeros((GAIN_ROWS, target.shape[3 - 1] - own), LOW)


def swap(values, axis, size, bit):
    return lax.ppermute(values, axis, [(i, i ^ (1 << bit)) for i in range(size)])


def bits_of(size):
    return size.bit_length() - 1


def gather(shard, size):
    held = [(0, shard)]
    for bit in reversed(range(bits_of(size))):
        held += [(r ^ (1 << bit), swap(block, "fsdp", size, bit)) for r, block in held]
    return [r for r, _ in held], [block for _, block in held]


def scatter_sum(keep, send, size):
    keep = keep + swap(send, "fsdp", size, 0)
    for bit in range(1, bits_of(size)):
        pairs = keep.reshape((keep.shape[0] // 2, 2) + keep.shape[1:])
        keep = pairs[:, 0] + swap(pairs[:, 1], "fsdp", size, bit)
    return keep[0]


def total_over(shard, size, me, axis, unit):
    steps = []
    for bit in range(bits_of(size)):
        length = shard.shape[axis]
        mine = (me >> bit) & 1
        halved = length % (2 * unit) == 0
        steps.append((bit, mine, halved))
        if halved:
            half = length // 2
            sent = lax.dynamic_slice_in_dim(shard, (1 - mine) * half, half, axis)
            kept = lax.dynamic_slice_in_dim(shard, mine * half, half, axis)
            shard = kept + swap(sent, "rep", size, bit)
        else:
            shard = shard + swap(shard, "rep", size, bit)
    for bit, mine, halved in reversed(steps):
        if halved:
            other = swap(shard, "rep", size, bit)
            shard = jnp.where(
                mine == 0,
                jnp.concatenate([shard, other], axis),
                jnp.concatenate([other, shard], axis),
            )
    return shard.astype(F32)


def shards(
    fsdp,
    rep,
    block_input,
    query_weight,
    key_weight,
    value_weight,
    out_weight,
    gate_weight,
    up_weight,
    down_weight,
    attn_gain,
    mlp_gain,
    segment_ids,
    doc_positions,
    out_cotangent,
):
    num_seqs, rows, width = block_input.shape
    assert num_seqs == 1
    keys = segment_ids.shape[1]
    me = lax.axis_index("fsdp")
    me_rep = lax.axis_index("rep")
    own = width // fsdp
    half = fsdp // 2
    qw, kw, ff = query_weight.shape[1], key_weight.shape[1], gate_weight.shape[1]
    pw = qw + 2 * kw
    table = jnp.stack([me, me_rep]).astype(jnp.int32)
    xt = block_input[0].T
    dyt = out_cotangent[0].T
    seg = segment_ids
    down_t = down_weight.T

    gains_own = jnp.zeros((GAIN_ROWS, pw), LOW)
    gains_own = gains_own.at[0, :own].set(attn_gain).at[1, :own].set(mlp_gain)
    proj_own = jnp.concatenate([query_weight, key_weight, value_weight], 1)
    rel, proj = gather(jnp.concatenate([proj_own, gains_own], 0), fsdp)

    frequency = 1.0 / THETA ** (jnp.arange(0, HD, 2).astype(F32) / HD)
    angles = doc_positions[0].astype(F32)[:, None] * frequency[None, :]
    angles = jnp.concatenate([angles] * 4, axis=-1)
    cosines, sines = jnp.cos(angles), jnp.sin(angles)

    n1, q, kv_own, gains = call(
        functools.partial(project_body, fsdp, rel),
        [((rows, width), LOW), ((rows, qw), LOW), ((rows, 2 * kw), LOW), ((GAIN_ROWS, width), F32)],
        [((fsdp, GAIN_ROWS, own), F32), ((fsdp, rows, own), LOW), ((rows, pw), F32)],
        2 * rows * width * pw,
        4 * width * pw,
        table, xt, cosines, sines, *proj,
    )
    _, kv = gather(kv_own, fsdp)
    _, outs = gather(out_weight, fsdp)
    _, gate_ups = gather(jnp.concatenate([gate_weight, up_weight], 1), fsdp)
    _, downs = gather(down_t, fsdp)

    head_scratch = [((QH, rows, HD), LOW), ((KVH, keys, HD), LOW), ((KVH, keys, HD), LOW),
                    ((keys, rows), F32)]
    ctx, lse, h1, n2 = call(
        functools.partial(attend_body, fsdp, rel),
        [((rows, qw), LOW), ((QH, 8, rows), F32), ((rows, width), F32), ((rows, width), LOW)],
        head_scratch + [((QH * HD, rows), F32), ((fsdp, rows, qw // fsdp), LOW)],
        4 * QH * HD * rows * keys * 4,
        4 * keys * rows,
        table, q, seg, xt, gains, *kv, *outs,
    )
    gp, up, act, down_keep, down_send = call(
        functools.partial(feed_body, fsdp, rel),
        [((rows, ff), F32), ((rows, ff), F32), ((rows, ff), LOW),
         ((half, width, ff // fsdp), LOW), ((half, width, ff // fsdp), LOW)],
        [((fsdp, rows, own), LOW)],
        6 * rows * width * ff,
        12 * width * ff,
        table, n2, dyt, *gate_ups,
    )
    yt, dgu, gu_keep, gu_send = call(
        functools.partial(feed_back_body, fsdp, rel),
        [((width, rows), LOW), ((rows, 2 * ff), LOW),
         ((2, half, own, ff), LOW), ((2, half, own, ff), LOW)],
        [((fsdp, rows, own), LOW)],
        8 * rows * width * ff,
        12 * width * ff,
        table, gp, up, act, dyt, h1, n2, *downs,
    )
    dh1, dctx, out_keep, out_send, mlp_gain_grad = call(
        functools.partial(stream_back_body, fsdp, rel),
        [((rows, width), F32), ((rows, qw), LOW), ((half, qw // fsdp, width), LOW),
         ((half, qw // fsdp, width), LOW), ((8, width), F32)],
        [((fsdp, rows, own), F32), ((fsdp, rows, qw // fsdp), LOW), ((fsdp, rows, qw // fsdp), F32)],
        4 * rows * width * ff,
        8 * width * ff,
        table, dgu, dyt, h1, gains, ctx, *gate_ups, *outs,
    )
    dqp, kv_keep, kv_send = call(
        functools.partial(attend_back_body, fsdp, rel),
        [((rows, qw), LOW), ((half, rows, 2 * kw), LOW), ((half, rows, 2 * kw), LOW)],
        head_scratch + [((QH, rows, HD), LOW), ((QH * HD + HD, rows), F32),
                        ((KVH, keys, HD), F32), ((KVH, keys, HD), F32)],
        10 * QH * HD * rows * keys * 4,
        4 * keys * rows,
        table, q, seg, lse, dctx, cosines, sines, *kv,
    )
    dkv = scatter_sum(kv_keep, kv_send, fsdp)
    dxt, proj_keep, proj_send = call(
        functools.partial(project_back_body, fsdp, rel),
        [((width, rows), LOW), ((half, own + GAIN_ROWS, pw), LOW), ((half, own + GAIN_ROWS, pw), LOW)],
        [((fsdp, rows, own), LOW), ((rows, pw), LOW), ((fsdp, rows, own), F32),
         ((fsdp, GAIN_ROWS, own), LOW)],
        4 * rows * width * pw,
        8 * width * pw,
        table, xt, n1, dqp, dkv, dh1, cosines, sines, gains, mlp_gain_grad, *proj,
    )

    def reduced(keep, send, axis, unit):
        shard = scatter_sum(keep, send, fsdp)
        return total_over(shard, rep, me_rep, axis, unit)

    down_total = reduced(down_keep, down_send, 0, 8)
    gate_total = reduced(gu_keep[0], gu_send[0], 1, 128)
    up_total = reduced(gu_keep[1], gu_send[1], 1, 128)
    out_total = reduced(out_keep, out_send, 0, 256)
    proj_total = reduced(proj_keep, proj_send, 0, 8)
    return (
        yt.T[None],
        dxt.T[None],
        proj_total[:own, :qw],
        proj_total[:own, qw : qw + kw],
        proj_total[:own, qw + kw :],
        out_total,
        gate_total,
        up_total,
        down_total.T,
        proj_total[own, :own],
        proj_total[own + 1, :own],
    )


def solution(mesh):
    in_specs = (
        P("rep", "fsdp", None),
        P("fsdp", None),
        P("fsdp", None),
        P("fsdp", None),
        P("fsdp", None),
        P("fsdp", None),
        P("fsdp", None),
        P("fsdp", None),
        P("fsdp"),
        P("fsdp"),
        P("rep", None),
        P("rep", "fsdp"),
        P("rep", "fsdp", None),
    )
    out_specs = (
        P("rep", "fsdp", None),
        P("rep", "fsdp", None),
        P("fsdp", None),
        P("fsdp", None),
        P("fsdp", None),
        P("fsdp", None),
        P("fsdp", None),
        P("fsdp", None),
        P("fsdp", None),
        P("fsdp"),
        P("fsdp"),
    )

    def body(*arrays):
        return shards(mesh.shape["fsdp"], mesh.shape["rep"], *arrays)

    return jax.shard_map(body, mesh=mesh, in_specs=in_specs, out_specs=out_specs, check_vma=False)
```

```python
import functools
import math

import jax
import jax.numpy as jnp
from jax import lax
from jax.experimental import pallas as pl
from jax.experimental.pallas import tpu as pltpu
from jax.sharding import PartitionSpec as P


QH = 9
KVH = 3
HD = 64
GROUP = QH // KVH

EPS = 1e-05
THETA = 100000.0
LOW = jnp.bfloat16
F32 = jnp.float32
GAIN_ROWS = 16
FSDP, REP = "fsdp", "rep"


VMEM_BYTES = 24 << 20
SMALL_BYTES = 8 << 20

VMEM = pl.BlockSpec(memory_space=pltpu.VMEM)


def dot(a, b):
    return lax.dot_general(a, b, (((1,), (0,)), ((), ())), preferred_element_type=F32)


def dot_nt(a, b):
    return lax.dot_general(a, b, (((1,), (1,)), ((), ())), preferred_element_type=F32)


def dot_tn(a, b):
    return lax.dot_general(a, b, (((0,), (0,)), ((), ())), preferred_element_type=F32)


def call(body, outs, scratch, flops, nbytes, *operands):
    return pl.pallas_call(
        body,
        out_shape=[jax.ShapeDtypeStruct(s, d) for s, d in outs],
        in_specs=[VMEM] * len(operands),
        out_specs=[VMEM] * len(outs),
        scratch_shapes=[pltpu.VMEM(s, d) for s, d in scratch],
        cost_estimate=pl.CostEstimate(flops=flops, bytes_accessed=nbytes, transcendentals=0),
        compiler_params=pltpu.CompilerParams(vmem_limit_bytes=VMEM_BYTES),
    )(*operands)


def inverse_root(stream):
    return lax.rsqrt(jnp.mean(stream * stream, axis=-1, keepdims=True) + EPS)


def norm_back(stream, gain, grad_norm):
    root = inverse_root(stream)
    scaled = grad_norm * gain
    grad_gain = jnp.sum(grad_norm * stream * root, axis=0, keepdims=True)
    inner = jnp.mean(scaled * stream, axis=-1, keepdims=True)
    return root * scaled - stream * (root * root * root) * inner, grad_gain


def turned(values, cosines, sines, sign):
    lane = lax.broadcasted_iota(jnp.int32, cosines.shape, 1) % HD
    parts = []
    for at in range(0, values.shape[1], 128):
        part = values[:, at : at + 128]
        half = jnp.where(lane < HD // 2, -pltpu.roll(part, 96, 1), pltpu.roll(part, 32, 1))
        parts.append(part * cosines + sign * half * sines)
    return jnp.concatenate(parts, 1) if len(parts) > 1 else parts[0]


def split_columns(values, target, count):
    width = values.shape[1] // count
    for j in range(count):
        target[j] = values[:, j * width : (j + 1) * width]


def join_columns(source, count):
    return jnp.concatenate([source[j] for j in range(count)], 1)


def prepare_body(xt_ref, position_ref, packed_ref, scaled_ref, cos_ref, sin_ref, own_ref):
    x = xt_ref[...].astype(F32).T
    scaled_ref[...] = x * inverse_root(x)
    rows, lanes = cos_ref.shape
    position = jnp.broadcast_to(position_ref[...].astype(F32), (8, rows)).T[:, 0:1]
    pair = lax.broadcasted_iota(jnp.int32, (8, lanes), 1) % (HD // 2)
    frequency = jnp.exp(pair.astype(F32) * (-2.0 / HD * math.log(THETA)))
    angles = position * frequency[0:1]
    cos_ref[...] = jnp.cos(angles)
    sin_ref[...] = jnp.sin(angles)
    own_ref[...] = packed_ref[...]


def project_kv_body(fsdp, rel, scaled_ref, cos_ref, sin_ref, *refs):
    weights, refs = refs[:fsdp], refs[fsdp:]
    n1_ref, kv_ref, gain_ref, gain_sc, n1_sc, acc_sc = refs
    me = lax.axis_index(FSDP)
    own = n1_ref.shape[1] // fsdp
    kw = kv_ref.shape[1] // 2
    for r, w in zip(rel, weights):
        gain_sc[me ^ r] = w[own : own + GAIN_ROWS, :own].astype(F32)
    gains = join_columns(gain_sc, fsdp)
    gain_ref[...] = gains
    n1 = (scaled_ref[...] * gains[0:1]).astype(LOW)
    n1_ref[...] = n1
    split_columns(n1, n1_sc, fsdp)
    for i, (r, w) in enumerate(zip(rel, weights)):
        part = dot(n1_sc[me ^ r], w[:own, :])
        acc_sc[...] = part if i == 0 else acc_sc[...] + part
    width = -(-kw // 128) * 128
    k = turned(acc_sc[:, :width], cos_ref[...], sin_ref[...], 1.0)[:, :kw].astype(LOW)
    kv_ref[...] = jnp.concatenate([k, acc_sc[:, kw:].astype(LOW)], 1)


def project_q_body(fsdp, rel, n1_ref, cos_ref, sin_ref, *refs):
    weights, refs = refs[:fsdp], refs[fsdp:]
    q_ref, n1_sc, acc_sc = refs
    me = lax.axis_index(FSDP)
    qw = q_ref.shape[1]
    split_columns(n1_ref[...], n1_sc, fsdp)
    acc_sc[:, qw:] = jnp.zeros((acc_sc.shape[0], acc_sc.shape[1] - qw), F32)
    for i, (r, w) in enumerate(zip(rel, weights)):
        part = dot(n1_sc[me ^ r], w[...])
        acc_sc[:, :qw] = part if i == 0 else acc_sc[:, :qw] + part
    q_ref[...] = turned(acc_sc[...], cos_ref[...], sin_ref[...], 1.0)[:, :qw].astype(LOW)


def load_heads(rel, me, heads, q_ref, kv_refs, q_sc, k_sc, v_sc):
    rows = q_ref.shape[0]
    for i, kh in enumerate(heads):
        for g in range(GROUP):
            h = kh * GROUP + g
            q_sc[i * GROUP + g] = q_ref[:, h * HD : (h + 1) * HD] * jnp.asarray(HD**-0.5, LOW)
        for r, kv in zip(rel, kv_refs):
            at = pl.ds(pl.multiple_of((me ^ r) * rows, rows), rows)
            k_sc[i, at, :] = kv[:, kh * HD : (kh + 1) * HD]
            v_sc[i, at, :] = kv[:, (KVH + kh) * HD : (KVH + kh + 1) * HD]


def limits(me, rows, seg_ref):
    keys = seg_ref.shape[1]
    seg = seg_ref[...].astype(F32)
    key_seg = jnp.broadcast_to(seg, (8, keys)).T[:, 0:1]
    query_seg = seg_ref[:, pl.ds(pl.multiple_of(me * rows, rows), rows)].astype(F32)
    key = lax.broadcasted_iota(jnp.int32, (keys, rows), 0)
    query = lax.broadcasted_iota(jnp.int32, (keys, rows), 1) + me * rows
    allowed = (key_seg == query_seg) & (key <= query)
    return jnp.where(allowed, jnp.finfo(F32).max, -1e30)


def attend_body(fsdp, rel, kh, q_ref, start_ref, *refs):
    kv_refs, refs = refs[:fsdp], refs[fsdp:]
    ctx_ref, lse_ref, refs = refs[0], refs[1], refs[2:]
    q_sc, k_sc, v_sc, ctx_t = refs[-4:]
    me = lax.axis_index(FSDP)
    rows = q_ref.shape[0]
    load_heads(rel, me, [kh], q_ref, kv_refs, q_sc, k_sc, v_sc)
    limit_ref = start_ref
    if kh == 0:
        limit_ref = refs[0]
        limit_ref[...] = limits(me, rows, start_ref)
    keys = k_sc[0]
    values_t = v_sc[0].T
    for g in range(GROUP):
        s = jnp.minimum(dot_nt(keys, q_sc[g]), limit_ref[...])
        top = jnp.max(s, axis=0, keepdims=True)
        e = jnp.exp(s - top)
        total = jnp.sum(e, axis=0, keepdims=True)
        lse_ref[g] = jnp.broadcast_to(top + jnp.log(total), (8, rows))
        ctx_t[g * HD : (g + 1) * HD, :] = dot(values_t, e.astype(LOW)) * (1.0 / total)
    ctx_ref[...] = ctx_t[...].T.astype(LOW)


def feed_body(fsdp, rel, xt_ref, gain_ref, dyt_ref, *refs):
    ctx_refs, refs = refs[:KVH], refs[KVH:]
    gate_refs, up_refs, refs = refs[:fsdp], refs[fsdp : 2 * fsdp], refs[2 * fsdp :]
    out_refs, refs = refs[:fsdp], refs[fsdp:]
    h1_ref, n2_ref, gp_ref, up_ref, act_ref = refs[:5]
    parts, (n2_sc, ctx_sc) = refs[5 : 5 + fsdp], refs[5 + fsdp :]
    me = lax.axis_index(FSDP)
    ff = gp_ref.shape[1]
    split_columns(jnp.concatenate([c[...] for c in ctx_refs], 1), ctx_sc, fsdp)
    h1 = xt_ref[...].astype(F32).T
    for r, w in zip(rel, out_refs):
        h1 = h1 + dot(ctx_sc[me ^ r], w[...])
    h1_ref[...] = h1
    n2 = (h1 * inverse_root(h1) * gain_ref[1:2]).astype(LOW)
    n2_ref[...] = n2
    split_columns(n2, n2_sc, fsdp)
    chunk = ff // 4

    @pl.loop(0, 4)
    def _(c):
        left = pl.ds(pl.multiple_of(c * chunk, chunk), chunk)
        gp = up = None
        for r, wg, wu in zip(rel, gate_refs, up_refs):
            n2 = n2_sc[me ^ r]
            g, u = dot(n2, wg[:, left]), dot(n2, wu[:, left])
            gp, up = (g, u) if gp is None else (gp + g, up + u)
        gp_ref[:, left] = gp
        up_ref[:, left] = up
        act_ref[:, left] = (gp * jax.nn.sigmoid(gp) * up).astype(LOW)

    rows = ff // fsdp
    for r in range(fsdp):
        at = pl.ds(pl.multiple_of((me ^ r) * rows, rows), rows)
        parts[r][...] = dot(dyt_ref[...], act_ref[:, at]).astype(LOW)


def feed_back_body(fsdp, rel, gp_ref, up_ref, act_ref, dyt_ref, h1_ref, n2_ref, *refs):
    down_refs, refs = refs[:fsdp], refs[fsdp:]
    yt_ref, dgu_ref, refs = refs[0], refs[1], refs[2:]
    gate_parts, up_parts, (n2_sc,) = refs[:fsdp], refs[fsdp : 2 * fsdp], refs[2 * fsdp :]
    me = lax.axis_index(FSDP)
    ff = gp_ref.shape[1]
    split_columns(n2_ref[...], n2_sc, fsdp)
    rows = ff // fsdp
    y = h1_ref[...]
    dy = dyt_ref[...].T
    for r, w in zip(rel, down_refs):
        at = pl.ds(pl.multiple_of((me ^ r) * rows, rows), rows)
        right = pl.ds(pl.multiple_of(ff + (me ^ r) * rows, rows), rows)
        y = y + dot_nt(act_ref[:, at], w[...])
        da = dot(dy, w[...])
        gp, up = gp_ref[:, at], up_ref[:, at]
        sg = jax.nn.sigmoid(gp)
        dgu_ref[:, at] = (da * up * sg * (1.0 + gp * (1.0 - sg))).astype(LOW)
        dgu_ref[:, right] = (da * gp * sg).astype(LOW)
    yt_ref[...] = y.T.astype(LOW)
    chunk = ff // 2

    @pl.loop(0, 2)
    def _(c):
        left = pl.ds(pl.multiple_of(c * chunk, chunk), chunk)
        right = pl.ds(pl.multiple_of(ff + c * chunk, chunk), chunk)
        for r in range(fsdp):
            n2 = n2_sc[me ^ r]
            gate_parts[r][:, left] = dot_tn(n2, dgu_ref[:, left]).astype(LOW)
            up_parts[r][:, left] = dot_tn(n2, dgu_ref[:, right]).astype(LOW)


def stream_back_body(fsdp, rel, dgu_ref, dyt_ref, h1_ref, gain_ref, *refs):
    ctx_refs, refs = refs[:KVH], refs[KVH:]
    gate_refs, up_refs, refs = refs[:fsdp], refs[fsdp : 2 * fsdp], refs[2 * fsdp :]
    out_refs, refs = refs[:fsdp], refs[fsdp:]
    dh1_ref, dctx_ref, gain_out = refs[:3]
    parts, (dn_sc, ctx_sc, dctx_sc) = refs[3 : 3 + fsdp], refs[3 + fsdp :]
    me = lax.axis_index(FSDP)
    ff = dgu_ref.shape[1] // 2
    for r, wg, wu in zip(rel, gate_refs, up_refs):
        dn_sc[me ^ r] = dot_nt(dgu_ref[:, :ff], wg[...]) + dot_nt(dgu_ref[:, ff:], wu[...])
    dv, grad_gain = norm_back(h1_ref[...], gain_ref[1:2], join_columns(dn_sc, fsdp))
    gain_out[...] = jnp.broadcast_to(grad_gain, gain_out.shape)
    dh1 = dyt_ref[...].astype(F32).T + dv
    dh1_ref[...] = dh1
    low = dh1.astype(LOW)
    for r, w in zip(rel, out_refs):
        dctx_sc[me ^ r] = dot_nt(low, w[...])
    dctx_ref[...] = join_columns(dctx_sc, fsdp).astype(LOW)
    split_columns(jnp.concatenate([c[...] for c in ctx_refs], 1), ctx_sc, fsdp)
    for r in range(fsdp):
        rows = ctx_sc.shape[2]
        parts[r][:rows, :] = dot_tn(ctx_sc[me ^ r], low).astype(LOW)
        parts[r][rows:, :] = jnp.zeros((parts[r].shape[0] - rows, low.shape[1]), LOW)


def attend_back_body(
    fsdp, rel, kh, q_ref, limit_ref, lse_ref, dctx_ref, cos_ref, sin_ref, *refs
):
    kv_refs, refs = refs[:fsdp], refs[fsdp:]
    earlier, refs = refs[: len(refs) - (1 + fsdp + 7)], refs[len(refs) - (1 + fsdp + 7) :]
    dqp_ref, parts = refs[0], refs[1 : 1 + fsdp]
    q_sc, k_sc, v_sc, dctx_sc, dq_t, dk_sc, dv_sc = refs[1 + fsdp :]
    me = lax.axis_index(FSDP)
    rows = q_ref.shape[0]
    load_heads(rel, me, [kh], q_ref, kv_refs, q_sc, k_sc, v_sc)
    for g in range(GROUP):
        h = kh * GROUP + g
        dctx_sc[g] = dctx_ref[:, h * HD : (h + 1) * HD]
    keys = k_sc[0]
    values = v_sc[0]
    keys_t = keys.T * jnp.asarray(HD**-0.5, LOW)
    for g in range(GROUP):
        s = jnp.minimum(dot_nt(keys, q_sc[g]), limit_ref[...])
        p = jnp.exp(s - lse_ref[g, 0:1, :])
        dv = dot(p.astype(LOW), dctx_sc[g])
        dp = dot_nt(values, dctx_sc[g])
        inner = jnp.sum(p * dp, axis=0, keepdims=True)
        ds = (p * (dp - inner)).astype(LOW)
        dk = dot(ds, q_sc[g])
        dk_sc[...] = dk if g == 0 else dk_sc[...] + dk
        dv_sc[...] = dv if g == 0 else dv_sc[...] + dv
        dq_t[g * HD : (g + 1) * HD, :] = dot(keys_t, ds)

    dq_t[GROUP * HD :, :] = jnp.zeros((HD, rows), F32)
    dq = turned(dq_t[...].T, cos_ref[...], sin_ref[...], -1.0)
    dqp_ref[...] = dq[:, : GROUP * HD].astype(LOW)
    for r in range(fsdp):
        at = pl.ds(pl.multiple_of((me ^ r) * rows, rows), rows)
        own = jnp.concatenate([dk_sc[at, :], dv_sc[at, :]], 1).astype(LOW)
        if earlier:
            blocks = [earlier[i * fsdp + r][...] for i in range(kh)] + [own]
            own = jnp.concatenate(
                [x[:, :HD] for x in blocks] + [x[:, HD:] for x in blocks], 1
            )
        parts[r][...] = own


def project_back_body(
    fsdp, rel, xt_ref, n1_ref, dkv_ref, dh1_ref, cos_ref, sin_ref, gain_ref,
    mlp_gain_ref, *refs
):
    dqp_refs, refs = refs[:KVH], refs[KVH:]
    q_weights, kv_weights, refs = refs[:fsdp], refs[fsdp : 2 * fsdp], refs[2 * fsdp :]
    dxt_ref, parts, (n1_sc, dproj_sc, dn_sc, gain_sc) = refs[0], refs[1 : 1 + fsdp], refs[1 + fsdp :]
    me = lax.axis_index(FSDP)
    own = n1_ref.shape[1] // fsdp
    kw = dkv_ref.shape[1] // 2
    dkv = dkv_ref[...]
    dk = jnp.concatenate([dkv[:, :kw].astype(F32), jnp.zeros((dkv.shape[0], 256 - kw), F32)], 1)
    dkp = turned(dk, cos_ref[...], sin_ref[...], -1.0)[:, :kw].astype(LOW)
    dproj_sc[...] = jnp.concatenate([d[...] for d in dqp_refs] + [dkp, dkv[:, kw:]], 1)
    qw = dproj_sc.shape[1] - 2 * kw
    for r, wq, wkv in zip(rel, q_weights, kv_weights):
        dn_sc[me ^ r] = dot_nt(dproj_sc[:, :qw], wq[...]) + dot_nt(dproj_sc[:, qw:], wkv[:own, :])
    dv, grad_gain = norm_back(xt_ref[...].astype(F32).T, gain_ref[0:1], join_columns(dn_sc, fsdp))
    dxt_ref[...] = (dh1_ref[...] + dv).T.astype(LOW)
    gains = jnp.concatenate(
        [grad_gain, mlp_gain_ref[0:1], jnp.zeros((GAIN_ROWS - 2, grad_gain.shape[1]), F32)], 0
    ).astype(LOW)
    split_columns(gains, gain_sc, fsdp)
    split_columns(n1_ref[...], n1_sc, fsdp)
    for r in range(fsdp):
        parts[r][:own, :] = dot_tn(n1_sc[me ^ r], dproj_sc[...]).astype(LOW)
        parts[r][own:, :own] = gain_sc[me ^ r]
        parts[r][own:, own:] = jnp.zeros((GAIN_ROWS, dproj_sc.shape[1] - own), LOW)


def pack_body(attn_ref, mlp_ref, k_ref, v_ref, packed_ref):
    own = k_ref.shape[0]
    packed_ref[:own, :] = jnp.concatenate([k_ref[...], v_ref[...]], 1)
    gains = jnp.concatenate(
        [
            attn_ref[...].astype(F32).reshape(1, own),
            mlp_ref[...].astype(F32).reshape(1, own),
            jnp.zeros((GAIN_ROWS - 2, own), F32),
        ],
        0,
    ).astype(LOW)
    packed_ref[own:, :own] = gains
    packed_ref[own:, own:] = jnp.zeros((GAIN_ROWS, packed_ref.shape[1] - own), LOW)


def swap(values, axis, size, bit):
    return lax.ppermute(values, axis, [(i, i ^ (1 << bit)) for i in range(size)])


def bits_of(size):
    return size.bit_length() - 1


def gather(shard, size, relay=None):
    held = [(0, shard)]
    for bit in reversed(range(bits_of(size))):
        if relay is not None and bit == bits_of(size) - 1 and bit > 0:
            held.append((1 << bit, relayed(shard, size, bit, *relay)))
        else:
            held += [(r ^ (1 << bit), swap(block, FSDP, size, bit)) for r, block in held]
    return [r for r, _ in held], [block for _, block in held]


def pick_body(axis, bit, whole_ref, half_ref):
    mine = (lax.axis_index(REP) >> bit) & 1
    half_ref[...] = whole_ref[half_at(axis, half_ref.shape[axis], mine)]


def relayed(shard, size, bit, rep, rep_bit, axis):
    shape = list(shard.shape)
    shape[axis] //= 2
    (sent,) = small(functools.partial(pick_body, axis, rep_bit), [(tuple(shape), LOW)], shard)
    direct = swap(sent, FSDP, size, bit)
    other = swap(direct, REP, rep, rep_bit)
    (block,) = small(
        functools.partial(join_body, axis, rep_bit),
        [(shard.shape, LOW)],
        direct, other,
    )
    return block


def small(body, outs, *operands):
    return pl.pallas_call(
        body,
        out_shape=[jax.ShapeDtypeStruct(shape, kind) for shape, kind in outs],
        in_specs=[VMEM] * len(operands),
        out_specs=[VMEM] * len(outs),
        compiler_params=pltpu.CompilerParams(vmem_limit_bytes=SMALL_BYTES),
    )(*operands)


def half_at(axis, half, index):
    at = pl.ds(pl.multiple_of(index * half, half), half)
    return (at, slice(None)) if axis == 0 else (slice(None), at)


def add_body(count, *refs):
    total = refs[0][...].astype(F32)
    for ref in refs[1:count]:
        total = total + ref[...].astype(F32)
    refs[count][...] = total.astype(refs[count].dtype)


def add_split_body(count, axis, bit, *refs):
    sent_ref, kept_ref = refs[count:]
    mine = (lax.axis_index(REP) >> bit) & 1
    half = kept_ref.shape[axis]
    for target, index in ((sent_ref, 1 - mine), (kept_ref, mine)):
        at = half_at(axis, half, index)
        total = refs[0][at].astype(F32)
        for ref in refs[1:count]:
            total = total + ref[at].astype(F32)
        target[...] = total.astype(LOW)


def join_body(axis, bit, own_ref, other_ref, joined_ref):
    mine = (lax.axis_index(REP) >> bit) & 1
    half = own_ref.shape[axis]
    joined_ref[half_at(axis, half, mine)] = own_ref[...].astype(joined_ref.dtype)
    joined_ref[half_at(axis, half, 1 - mine)] = other_ref[...].astype(joined_ref.dtype)


def join_proj_body(own, qw, kw, own_ref, other_ref, q_ref, k_ref, v_ref, attn_ref, mlp_ref, joined):
    mine = lax.axis_index(REP) & 1
    half = own_ref.shape[0]
    joined[half_at(0, half, mine)] = own_ref[...].astype(F32)
    joined[half_at(0, half, 1 - mine)] = other_ref[...].astype(F32)
    q_ref[...] = joined[:own, :qw]
    k_ref[...] = joined[:own, qw : qw + kw]
    v_ref[...] = joined[:own, qw + kw :]
    attn_ref[...] = joined[own : own + 1, :own].reshape(own)
    mlp_ref[...] = joined[own + 1 : own + 2, :own].reshape(own)


def scatter_terms(parts, size):
    for bit in range(bits_of(size)):
        terms = []
        for i in range(0, len(parts), 2):
            arrived = swap(parts[i + 1], FSDP, size, bit)
            if len(parts) > 2 and i % 4 == 2:
                (arrived,) = small(
                    functools.partial(add_body, 2),
                    [(arrived.shape, LOW)],
                    parts[i], arrived,
                )
                terms.append(arrived)
            else:
                terms.append((parts[i], arrived))
        if len(terms) == 1:
            return flat(terms[0])
        parts = terms
    return flat(parts[0])


def flat(term):
    return sum((flat(t) for t in term), []) if isinstance(term, tuple) else [term]


def total_over(terms, size, halvings, axis):
    shape = list(terms[0].shape)
    for bit in range(bits_of(size)):
        if bit < halvings:
            shape[axis] //= 2
            sent, kept = small(
                functools.partial(add_split_body, len(terms), axis, bit),
                [(tuple(shape), LOW)] * 2,
                *terms,
            )
            terms = [kept, swap(sent, REP, size, bit)]
        else:
            (total,) = small(functools.partial(add_body, len(terms)), [(tuple(shape), LOW)], *terms)
            terms = [total, swap(total, REP, size, bit)]
    (total,) = small(
        functools.partial(add_body, len(terms)),
        [(tuple(shape), F32 if halvings == 0 else LOW)],
        *terms,
    )
    for bit in reversed(range(1, halvings)):
        shape[axis] *= 2
        (total,) = small(
            functools.partial(join_body, axis, bit),
            [(tuple(shape), LOW)],
            total, swap(total, REP, size, bit),
        )
    return total


def join_crop_body(bit, own_ref, other_ref, cropped_ref, joined):
    mine = (lax.axis_index(REP) >> bit) & 1
    half = own_ref.shape[0]
    joined[half_at(0, half, mine)] = own_ref[...].astype(joined.dtype)
    joined[half_at(0, half, 1 - mine)] = other_ref[...].astype(joined.dtype)
    cropped_ref[...] = joined[: cropped_ref.shape[0], :]


def restored(shard, size, axis, crop=None):
    shape = list(shard.shape)
    shape[axis] *= 2
    if crop is not None:
        run = pl.pallas_call(
            functools.partial(join_crop_body, 0),
            name="j",
            out_shape=jax.ShapeDtypeStruct((crop, shape[1]), F32),
            in_specs=[VMEM, VMEM],
            out_specs=VMEM,
            scratch_shapes=[pltpu.VMEM(tuple(shape), F32)],
            compiler_params=pltpu.CompilerParams(vmem_limit_bytes=SMALL_BYTES),
        )
        return run(shard, swap(shard, REP, size, 0))
    return small(
        functools.partial(join_body, axis, 0),
        [(tuple(shape), F32)],
        shard, swap(shard, REP, size, 0),
    )[0]


def shards(
    fsdp,
    rep,
    block_input,
    query_weight,
    key_weight,
    value_weight,
    out_weight,
    gate_weight,
    up_weight,
    down_weight,
    attn_gain,
    mlp_gain,
    segment_ids,
    doc_positions,
    out_cotangent,
):
    num_seqs, rows, width = block_input.shape
    assert num_seqs == 1
    keys = segment_ids.shape[1]
    own = width // fsdp
    qw, kw, ff = query_weight.shape[1], key_weight.shape[1], gate_weight.shape[1]
    pw = qw + 2 * kw
    xt = block_input[0].T
    dyt = out_cotangent[0].T
    seg = segment_ids
    down_t = down_weight.T

    packed = pl.pallas_call(
        pack_body,
        name="p",
        out_shape=jax.ShapeDtypeStruct((own + GAIN_ROWS, 2 * kw), LOW),
        in_specs=[VMEM] * 4,
        out_specs=VMEM,
        compiler_params=pltpu.CompilerParams(vmem_limit_bytes=60 << 20),
    )(attn_gain, mlp_gain, key_weight, value_weight)
    rel, wkv = gather(packed, fsdp)
    _, wq = gather(query_weight, fsdp)

    scaled, cosines, sines, packed_here = call(
        prepare_body,
        [((rows, width), F32), ((rows, 128), F32), ((rows, 128), F32), (packed.shape, LOW)],
        [],
        100 * rows * width,
        8 * rows * width,
        xt, doc_positions, packed,
    )
    wkv = [packed_here] + wkv[1:]

    n1, kv_own, gains = call(
        functools.partial(project_kv_body, fsdp, rel),
        [((rows, width), LOW), ((rows, 2 * kw), LOW), ((GAIN_ROWS, width), F32)],
        [((fsdp, GAIN_ROWS, own), F32), ((fsdp, rows, own), LOW), ((rows, 2 * kw), F32)],
        2 * rows * width * 2 * kw,
        4 * width * pw,
        scaled, cosines, sines, *wkv,
    )
    (q,) = call(
        functools.partial(project_q_body, fsdp, rel),
        [((rows, qw), LOW)],
        [((fsdp, rows, own), LOW), ((rows, -(-qw // 128) * 128), F32)],
        2 * rows * width * qw,
        4 * width * qw,
        n1, cosines, sines, *wq,
    )
    _, kv = gather(kv_own, fsdp)
    many = rep > 1
    _, outs = gather(out_weight, fsdp)
    _, gates = gather(gate_weight, fsdp, (rep, 0, 1) if many else None)
    _, ups = gather(up_weight, fsdp, (rep, min(1, bits_of(rep) - 1), 1) if many else None)
    _, downs = gather(down_t, fsdp)

    def head_scratch(count):
        return [((count * GROUP, rows, HD), LOW), ((count, keys, HD), LOW), ((count, keys, HD), LOW)]

    ctxs, lses, limit = [], [], None
    for kh in range(KVH):
        ctx, lse, *made = call(
            functools.partial(attend_body, fsdp, rel, kh),
            [((rows, GROUP * HD), LOW), ((GROUP, 8, rows), F32)]
            + [((keys, rows), F32)] * (kh == 0),
            head_scratch(1) + [((GROUP * HD, rows), F32)],
            4 * GROUP * HD * rows * keys * 4,
            4 * keys * rows,
            q, seg if kh == 0 else limit, *kv,
        )
        ctxs.append(ctx)
        lses.append(lse)
        limit = made[0] if kh == 0 else limit
    h1, n2, gp, up, act, *down_parts = call(
        functools.partial(feed_body, fsdp, rel),
        [((rows, width), F32), ((rows, width), LOW),
         ((rows, ff), F32), ((rows, ff), F32), ((rows, ff), LOW)]
        + [((width, ff // fsdp), LOW)] * fsdp,
        [((fsdp, rows, own), LOW), ((fsdp, rows, qw // fsdp), LOW)],
        6 * rows * width * ff,
        12 * width * ff,
        xt, gains, dyt, *ctxs, *gates, *ups, *outs,
    )
    yt, dgu, *gate_up_parts = call(
        functools.partial(feed_back_body, fsdp, rel),
        [((width, rows), LOW), ((rows, 2 * ff), LOW)] + [((own, ff), LOW)] * (2 * fsdp),
        [((fsdp, rows, own), LOW)],
        8 * rows * width * ff,
        12 * width * ff,
        gp, up, act, dyt, h1, n2, *downs,
    )
    dh1, dctx, mlp_gain_grad, *out_parts = call(
        functools.partial(stream_back_body, fsdp, rel),
        [((rows, width), F32), ((rows, qw), LOW), ((8, width), F32)]
        + [((-(-qw // fsdp // 32) * 32, width), LOW)] * fsdp,
        [((fsdp, rows, own), F32), ((fsdp, rows, qw // fsdp), LOW), ((fsdp, rows, qw // fsdp), F32)],
        4 * rows * width * ff,
        8 * width * ff,
        dgu, dyt, h1, gains, *ctxs, *gates, *ups, *outs,
    )
    dqps, kv_parts, earlier = [], [], []
    for kh in range(KVH):
        last = kh == KVH - 1
        dqp, *kv_parts = call(
            functools.partial(attend_back_body, fsdp, rel, kh),
            [((rows, GROUP * HD), LOW)] + [((rows, 2 * (kw if last else HD)), LOW)] * fsdp,
            head_scratch(1) + [((GROUP, rows, HD), LOW), ((GROUP * HD + HD, rows), F32),
                               ((keys, HD), F32), ((keys, HD), F32)],
            10 * GROUP * HD * rows * keys * 4,
            4 * keys * rows,
            q, limit, lses[kh], dctx, cosines, sines, *kv, *(earlier if last else ()),
        )
        dqps.append(dqp)
        earlier += kv_parts
    dkv_terms = scatter_terms(kv_parts, fsdp)
    (dkv,) = small(functools.partial(add_body, len(dkv_terms)), [((rows, 2 * kw), LOW)], *dkv_terms)
    dxt, *proj_parts = call(
        functools.partial(project_back_body, fsdp, rel),
        [((width, rows), LOW)] + [((own + GAIN_ROWS, pw), LOW)] * fsdp,
        [((fsdp, rows, own), LOW), ((rows, pw), LOW), ((fsdp, rows, own), F32),
         ((fsdp, GAIN_ROWS, own), LOW)],
        4 * rows * width * pw,
        8 * width * pw,
        xt, n1, dkv, dh1, cosines, sines, gains, mlp_gain_grad, *dqps, *wq, *wkv,
    )

    def reduced(parts, halvings, axis):
        terms = scatter_terms(parts, fsdp)
        return total_over(terms, rep, min(halvings, bits_of(rep)), axis)

    down_shard = reduced(down_parts, 1, 0)
    down_total = restored(down_shard, rep, 0)
    gate_shard = reduced(gate_up_parts[:fsdp], 2, 1)
    gate_total = restored(gate_shard, rep, 1)
    up_shard = reduced(gate_up_parts[fsdp:], 2, 1)
    up_total = restored(up_shard, rep, 1)
    out_shard = reduced(out_parts, 1, 0)
    out_total = restored(out_shard, rep, 0, qw // fsdp)
    proj_shard = reduced(proj_parts, 1, 0)
    other = swap(proj_shard, REP, rep, 0)
    run = pl.pallas_call(
        functools.partial(join_proj_body, own, qw, kw),
        name="j",
        out_shape=[
            jax.ShapeDtypeStruct(shape, F32)
            for shape in ((own, qw), (own, kw), (own, kw), (own,), (own,))
        ],
        in_specs=[VMEM, VMEM],
        out_specs=[VMEM] * 5,
        scratch_shapes=[pltpu.VMEM((own + GAIN_ROWS, pw), F32)],
        compiler_params=pltpu.CompilerParams(vmem_limit_bytes=SMALL_BYTES),
    )
    grad_q, grad_k, grad_v, grad_attn_gain, grad_mlp_gain = run(proj_shard, other)
    return (
        yt.T[None],
        dxt.T[None],
        grad_q,
        grad_k,
        grad_v,
        out_total,
        gate_total,
        up_total,
        down_total.T,
        grad_attn_gain,
        grad_mlp_gain,
    )


def solution(mesh):
    in_specs = (
        P(REP, FSDP, None),
        P(FSDP, None),
        P(FSDP, None),
        P(FSDP, None),
        P(FSDP, None),
        P(FSDP, None),
        P(FSDP, None),
        P(FSDP, None),
        P(FSDP),
        P(FSDP),
        P(REP, None),
        P(REP, FSDP),
        P(REP, FSDP, None),
    )
    out_specs = (
        P(REP, FSDP, None),
        P(REP, FSDP, None),
        P(FSDP, None),
        P(FSDP, None),
        P(FSDP, None),
        P(FSDP, None),
        P(FSDP, None),
        P(FSDP, None),
        P(FSDP, None),
        P(FSDP),
        P(FSDP),
    )

    def body(*arrays):
        return shards(mesh.shape[FSDP], mesh.shape[REP], *arrays)

    return jax.shard_map(body, mesh=mesh, in_specs=in_specs, out_specs=out_specs, check_vma=False)
```

```python
import functools
import math

import jax
import jax.numpy as jnp
from jax import lax
from jax.experimental import pallas as pl
from jax.experimental.pallas import tpu as pltpu
from jax.sharding import PartitionSpec as P


QH = 9
KVH = 3
HD = 64
GROUP = QH // KVH

EPS = 1e-05
THETA = 100000.0
LOW = jnp.bfloat16
F32 = jnp.float32
GAIN_ROWS = 16
FSDP, REP = "fsdp", "rep"


VMEM_BYTES = 24 << 20
SMALL_BYTES = 8 << 20

VMEM = pl.BlockSpec(memory_space=pltpu.VMEM)


def dot(a, b):
    return lax.dot_general(a, b, (((1,), (0,)), ((), ())), preferred_element_type=F32)


def dot_nt(a, b):
    return lax.dot_general(a, b, (((1,), (1,)), ((), ())), preferred_element_type=F32)


def dot_tn(a, b):
    return lax.dot_general(a, b, (((0,), (0,)), ((), ())), preferred_element_type=F32)


def call(body, outs, scratch, flops, nbytes, *operands):
    return pl.pallas_call(
        body,
        out_shape=[jax.ShapeDtypeStruct(s, d) for s, d in outs],
        in_specs=[VMEM] * len(operands),
        out_specs=[VMEM] * len(outs),
        scratch_shapes=[pltpu.VMEM(s, d) for s, d in scratch],
        cost_estimate=pl.CostEstimate(flops=flops, bytes_accessed=nbytes, transcendentals=0),
        compiler_params=pltpu.CompilerParams(vmem_limit_bytes=VMEM_BYTES),
    )(*operands)


def inverse_root(stream):
    return lax.rsqrt(jnp.mean(stream * stream, axis=-1, keepdims=True) + EPS)


def norm_back(stream, gain, grad_norm):
    root = inverse_root(stream)
    scaled = grad_norm * gain
    grad_gain = jnp.sum(grad_norm * stream * root, axis=0, keepdims=True)
    inner = jnp.mean(scaled * stream, axis=-1, keepdims=True)
    return root * scaled - stream * (root * root * root) * inner, grad_gain


def turned(values, cosines, sines, sign):
    lane = lax.broadcasted_iota(jnp.int32, cosines.shape, 1) % HD
    parts = []
    for at in range(0, values.shape[1], 128):
        part = values[:, at : at + 128]
        half = jnp.where(lane < HD // 2, -pltpu.roll(part, 96, 1), pltpu.roll(part, 32, 1))
        parts.append(part * cosines + sign * half * sines)
    return jnp.concatenate(parts, 1) if len(parts) > 1 else parts[0]


def split_columns(values, target, count):
    width = values.shape[1] // count
    for j in range(count):
        target[j] = values[:, j * width : (j + 1) * width]


def join_columns(source, count):
    return jnp.concatenate([source[j] for j in range(count)], 1)


def prepare_body(xt_ref, position_ref, packed_ref, scaled_ref, cos_ref, sin_ref, own_ref):
    x = xt_ref[...].astype(F32).T
    scaled_ref[...] = x * inverse_root(x)
    rows, lanes = cos_ref.shape
    position = jnp.broadcast_to(position_ref[...].astype(F32), (8, rows)).T[:, 0:1]
    pair = lax.broadcasted_iota(jnp.int32, (8, lanes), 1) % (HD // 2)
    frequency = jnp.exp(pair.astype(F32) * (-2.0 / HD * math.log(THETA)))
    angles = position * frequency[0:1]
    cos_ref[...] = jnp.cos(angles)
    sin_ref[...] = jnp.sin(angles)
    own_ref[...] = packed_ref[...]


def project_kv_body(fsdp, rel, scaled_ref, cos_ref, sin_ref, *refs):
    weights, refs = refs[:fsdp], refs[fsdp:]
    n1_ref, kv_ref, gain_ref, gain_sc, n1_sc, acc_sc = refs
    me = lax.axis_index(FSDP)
    own = n1_ref.shape[1] // fsdp
    kw = kv_ref.shape[1] // 2
    for r, w in zip(rel, weights):
        gain_sc[me ^ r] = w[own : own + GAIN_ROWS, :own].astype(F32)
    gains = join_columns(gain_sc, fsdp)
    gain_ref[...] = gains
    n1 = (scaled_ref[...] * gains[0:1]).astype(LOW)
    n1_ref[...] = n1
    split_columns(n1, n1_sc, fsdp)
    for i, (r, w) in enumerate(zip(rel, weights)):
        part = dot(n1_sc[me ^ r], w[:own, :])
        acc_sc[...] = part if i == 0 else acc_sc[...] + part
    width = -(-kw // 128) * 128
    k = turned(acc_sc[:, :width], cos_ref[...], sin_ref[...], 1.0)[:, :kw].astype(LOW)
    kv_ref[...] = jnp.concatenate([k, acc_sc[:, kw:].astype(LOW)], 1)


def project_q_body(fsdp, rel, n1_ref, cos_ref, sin_ref, *refs):
    weights, refs = refs[:fsdp], refs[fsdp:]
    q_ref, n1_sc, acc_sc = refs
    me = lax.axis_index(FSDP)
    qw = q_ref.shape[1]
    split_columns(n1_ref[...], n1_sc, fsdp)
    acc_sc[:, qw:] = jnp.zeros((acc_sc.shape[0], acc_sc.shape[1] - qw), F32)
    for i, (r, w) in enumerate(zip(rel, weights)):
        part = dot(n1_sc[me ^ r], w[...])
        acc_sc[:, :qw] = part if i == 0 else acc_sc[:, :qw] + part
    q_ref[...] = turned(acc_sc[...], cos_ref[...], sin_ref[...], 1.0)[:, :qw].astype(LOW)


def load_heads(rel, me, heads, q_ref, kv_refs, q_sc, k_sc, v_sc):
    rows = q_ref.shape[0]
    for i, kh in enumerate(heads):
        for g in range(GROUP):
            h = kh * GROUP + g
            q_sc[i * GROUP + g] = q_ref[:, h * HD : (h + 1) * HD] * jnp.asarray(HD**-0.5, LOW)
        for r, kv in zip(rel, kv_refs):
            at = pl.ds(pl.multiple_of((me ^ r) * rows, rows), rows)
            k_sc[i, at, :] = kv[:, kh * HD : (kh + 1) * HD]
            v_sc[i, at, :] = kv[:, (KVH + kh) * HD : (KVH + kh + 1) * HD]


def limits(me, rows, seg_ref):
    keys = seg_ref.shape[1]
    seg = seg_ref[...].astype(F32)
    key_seg = jnp.broadcast_to(seg, (8, keys)).T[:, 0:1]
    query_seg = seg_ref[:, pl.ds(pl.multiple_of(me * rows, rows), rows)].astype(F32)
    key = lax.broadcasted_iota(jnp.int32, (keys, rows), 0)
    query = lax.broadcasted_iota(jnp.int32, (keys, rows), 1) + me * rows
    allowed = (key_seg == query_seg) & (key <= query)
    return jnp.where(allowed, jnp.finfo(F32).max, -1e30)


def attend_body(fsdp, rel, kh, q_ref, start_ref, *refs):
    kv_refs, refs = refs[:fsdp], refs[fsdp:]
    ctx_ref, lse_ref, refs = refs[0], refs[1], refs[2:]
    q_sc, k_sc, v_sc, ctx_t = refs[-4:]
    me = lax.axis_index(FSDP)
    rows = q_ref.shape[0]
    load_heads(rel, me, [kh], q_ref, kv_refs, q_sc, k_sc, v_sc)
    limit_ref = start_ref
    if kh == 0:
        limit_ref = refs[0]
        limit_ref[...] = limits(me, rows, start_ref)
    keys = k_sc[0]
    values_t = v_sc[0].T
    for g in range(GROUP):
        s = jnp.minimum(dot_nt(keys, q_sc[g]), limit_ref[...])
        top = jnp.max(s, axis=0, keepdims=True)
        e = jnp.exp(s - top)
        total = jnp.sum(e, axis=0, keepdims=True)
        lse_ref[g] = jnp.broadcast_to(top + jnp.log(total), (8, rows))
        ctx_t[g * HD : (g + 1) * HD, :] = dot(values_t, e.astype(LOW)) * (1.0 / total)
    ctx_ref[...] = ctx_t[...].T.astype(LOW)


def feed_body(fsdp, rel, xt_ref, gain_ref, dyt_ref, *refs):
    ctx_refs, refs = refs[:KVH], refs[KVH:]
    gate_refs, up_refs, refs = refs[:fsdp], refs[fsdp : 2 * fsdp], refs[2 * fsdp :]
    out_refs, refs = refs[:fsdp], refs[fsdp:]
    h1_ref, n2_ref, gp_ref, up_ref, act_ref = refs[:5]
    parts, (n2_sc, ctx_sc) = refs[5 : 5 + fsdp // 2], refs[5 + fsdp // 2 :]
    me = lax.axis_index(FSDP)
    ff = gp_ref.shape[1]
    split_columns(jnp.concatenate([c[...] for c in ctx_refs], 1), ctx_sc, fsdp)
    h1 = xt_ref[...].astype(F32).T
    for r, w in zip(rel, out_refs):
        h1 = h1 + dot(ctx_sc[me ^ r], w[...])
    h1_ref[...] = h1
    n2 = (h1 * inverse_root(h1) * gain_ref[1:2]).astype(LOW)
    n2_ref[...] = n2
    split_columns(n2, n2_sc, fsdp)
    chunk = ff // 4

    @pl.loop(0, 4)
    def _(c):
        left = pl.ds(pl.multiple_of(c * chunk, chunk), chunk)
        gp = up = None
        for r, wg, wu in zip(rel, gate_refs, up_refs):
            n2 = n2_sc[me ^ r]
            g, u = dot(n2, wg[:, left]), dot(n2, wu[:, left])
            gp, up = (g, u) if gp is None else (gp + g, up + u)
        gp_ref[:, left] = gp
        up_ref[:, left] = up
        act_ref[:, left] = (gp * jax.nn.sigmoid(gp) * up).astype(LOW)

    down_parts(fsdp, fsdp // 2, dyt_ref, act_ref, parts)


def down_parts(fsdp, first, dyt_ref, act_ref, parts):
    me = lax.axis_index(FSDP)
    rows = act_ref.shape[1] // fsdp
    for i, part in enumerate(parts):
        at = pl.ds(pl.multiple_of((me ^ (first + i)) * rows, rows), rows)
        part[...] = dot(dyt_ref[...], act_ref[:, at]).astype(LOW)


def down_rest_body(fsdp, dyt_ref, act_ref, *parts):
    down_parts(fsdp, 0, dyt_ref, act_ref, parts)


def feed_back_body(fsdp, rel, gp_ref, up_ref, act_ref, dyt_ref, h1_ref, n2_ref, *refs):
    down_refs, refs = refs[:fsdp], refs[fsdp:]
    yt_ref, dgu_ref, refs = refs[0], refs[1], refs[2:]
    parts, (n2_sc,) = refs[: fsdp // 2], refs[fsdp // 2 :]
    me = lax.axis_index(FSDP)
    ff = gp_ref.shape[1]
    split_columns(n2_ref[...], n2_sc, fsdp)
    rows = ff // fsdp
    y = h1_ref[...]
    dy = dyt_ref[...].T
    for r, w in zip(rel, down_refs):
        at = pl.ds(pl.multiple_of((me ^ r) * rows, rows), rows)
        right = pl.ds(pl.multiple_of(ff + (me ^ r) * rows, rows), rows)
        y = y + dot_nt(act_ref[:, at], w[...])
        da = dot(dy, w[...])
        gp, up = gp_ref[:, at], up_ref[:, at]
        sg = jax.nn.sigmoid(gp)
        dgu_ref[:, at] = (da * up * sg * (1.0 + gp * (1.0 - sg))).astype(LOW)
        dgu_ref[:, right] = (da * gp * sg).astype(LOW)
    yt_ref[...] = y.T.astype(LOW)
    gate_up_parts([(0, fsdp // 2 + i, p) for i, p in enumerate(parts)], dgu_ref, n2_sc)


def gate_up_parts(targets, dgu_ref, n2_sc):
    me = lax.axis_index(FSDP)
    ff = dgu_ref.shape[1] // 2
    chunk = ff // 2

    @pl.loop(0, 2)
    def _(c):
        at = pl.ds(pl.multiple_of(c * chunk, chunk), chunk)
        for which, r, part in targets:
            source = pl.ds(pl.multiple_of(which * ff + c * chunk, chunk), chunk)
            part[:, at] = dot_tn(n2_sc[me ^ r], dgu_ref[:, source]).astype(LOW)


def gate_up_rest_body(fsdp, n2_ref, dgu_ref, *refs):
    n2_sc = refs[-1]
    split_columns(n2_ref[...], n2_sc, fsdp)
    targets = [(1, fsdp // 2 + i) for i in range(fsdp // 2)]
    targets += [(which, r) for which in range(2) for r in range(fsdp // 2)]
    targets = [(which, r, part) for (which, r), part in zip(targets, refs)]
    gate_up_parts(targets, dgu_ref, n2_sc)


def stream_back_body(fsdp, rel, dgu_ref, dyt_ref, h1_ref, gain_ref, *refs):
    ctx_refs, refs = refs[:KVH], refs[KVH:]
    gate_refs, up_refs, refs = refs[:fsdp], refs[fsdp : 2 * fsdp], refs[2 * fsdp :]
    out_refs, refs = refs[:fsdp], refs[fsdp:]
    dh1_ref, dctx_ref, gain_out = refs[:3]
    parts, (dn_sc, ctx_sc, dctx_sc) = refs[3 : 3 + fsdp], refs[3 + fsdp :]
    me = lax.axis_index(FSDP)
    ff = dgu_ref.shape[1] // 2
    for r, wg, wu in zip(rel, gate_refs, up_refs):
        dn_sc[me ^ r] = dot_nt(dgu_ref[:, :ff], wg[...]) + dot_nt(dgu_ref[:, ff:], wu[...])
    dv, grad_gain = norm_back(h1_ref[...], gain_ref[1:2], join_columns(dn_sc, fsdp))
    gain_out[...] = jnp.broadcast_to(grad_gain, gain_out.shape)
    dh1 = dyt_ref[...].astype(F32).T + dv
    dh1_ref[...] = dh1
    low = dh1.astype(LOW)
    for r, w in zip(rel, out_refs):
        dctx_sc[me ^ r] = dot_nt(low, w[...])
    dctx_ref[...] = join_columns(dctx_sc, fsdp).astype(LOW)
    split_columns(jnp.concatenate([c[...] for c in ctx_refs], 1), ctx_sc, fsdp)
    for r in range(fsdp):
        rows = ctx_sc.shape[2]
        parts[r][:rows, :] = dot_tn(ctx_sc[me ^ r], low).astype(LOW)
        parts[r][rows:, :] = jnp.zeros((parts[r].shape[0] - rows, low.shape[1]), LOW)


def attend_back_body(
    fsdp, rel, kh, q_ref, limit_ref, lse_ref, dctx_ref, cos_ref, sin_ref, *refs
):
    kv_refs, refs = refs[:fsdp], refs[fsdp:]
    earlier, refs = refs[: len(refs) - (1 + fsdp + 7)], refs[len(refs) - (1 + fsdp + 7) :]
    dqp_ref, parts = refs[0], refs[1 : 1 + fsdp]
    q_sc, k_sc, v_sc, dctx_sc, dq_t, dk_sc, dv_sc = refs[1 + fsdp :]
    me = lax.axis_index(FSDP)
    rows = q_ref.shape[0]
    load_heads(rel, me, [kh], q_ref, kv_refs, q_sc, k_sc, v_sc)
    for g in range(GROUP):
        h = kh * GROUP + g
        dctx_sc[g] = dctx_ref[:, h * HD : (h + 1) * HD]
    keys = k_sc[0]
    values = v_sc[0]
    keys_t = keys.T * jnp.asarray(HD**-0.5, LOW)
    for g in range(GROUP):
        s = jnp.minimum(dot_nt(keys, q_sc[g]), limit_ref[...])
        p = jnp.exp(s - lse_ref[g, 0:1, :])
        dv = dot(p.astype(LOW), dctx_sc[g])
        dp = dot_nt(values, dctx_sc[g])
        inner = jnp.sum(p * dp, axis=0, keepdims=True)
        ds = (p * (dp - inner)).astype(LOW)
        dk = dot(ds, q_sc[g])
        dk_sc[...] = dk if g == 0 else dk_sc[...] + dk
        dv_sc[...] = dv if g == 0 else dv_sc[...] + dv
        dq_t[g * HD : (g + 1) * HD, :] = dot(keys_t, ds)

    dq_t[GROUP * HD :, :] = jnp.zeros((HD, rows), F32)
    dq = turned(dq_t[...].T, cos_ref[...], sin_ref[...], -1.0)
    dqp_ref[...] = dq[:, : GROUP * HD].astype(LOW)
    for r in range(fsdp):
        at = pl.ds(pl.multiple_of((me ^ r) * rows, rows), rows)
        own = jnp.concatenate([dk_sc[at, :], dv_sc[at, :]], 1).astype(LOW)
        if earlier:
            blocks = [earlier[i * fsdp + r][...] for i in range(kh)] + [own]
            own = jnp.concatenate(
                [x[:, :HD] for x in blocks] + [x[:, HD:] for x in blocks], 1
            )
        parts[r][...] = own


def project_back_body(
    fsdp, rel, xt_ref, n1_ref, dkv_ref, dh1_ref, cos_ref, sin_ref, gain_ref,
    mlp_gain_ref, *refs
):
    dqp_refs, refs = refs[:KVH], refs[KVH:]
    q_weights, kv_weights, refs = refs[:fsdp], refs[fsdp : 2 * fsdp], refs[2 * fsdp :]
    dxt_ref, dproj_sc, gains_ref, refs = refs[0], refs[1], refs[2], refs[3:]
    parts, (n1_sc, dn_sc, gain_sc) = refs[: fsdp // 2], refs[fsdp // 2 :]
    me = lax.axis_index(FSDP)
    own = n1_ref.shape[1] // fsdp
    kw = dkv_ref.shape[1] // 2
    dkv = dkv_ref[...]
    dk = jnp.concatenate([dkv[:, :kw].astype(F32), jnp.zeros((dkv.shape[0], 256 - kw), F32)], 1)
    dkp = turned(dk, cos_ref[...], sin_ref[...], -1.0)[:, :kw].astype(LOW)
    dproj_sc[...] = jnp.concatenate([d[...] for d in dqp_refs] + [dkp, dkv[:, kw:]], 1)
    qw = dproj_sc.shape[1] - 2 * kw
    for r, wq, wkv in zip(rel, q_weights, kv_weights):
        dn_sc[me ^ r] = dot_nt(dproj_sc[:, :qw], wq[...]) + dot_nt(dproj_sc[:, qw:], wkv[:own, :])
    dv, grad_gain = norm_back(xt_ref[...].astype(F32).T, gain_ref[0:1], join_columns(dn_sc, fsdp))
    dxt_ref[...] = (dh1_ref[...] + dv).T.astype(LOW)
    gains = jnp.concatenate(
        [grad_gain, mlp_gain_ref[0:1], jnp.zeros((GAIN_ROWS - 2, grad_gain.shape[1]), F32)], 0
    ).astype(LOW)
    gains_ref[...] = gains
    proj_parts(fsdp, fsdp // 2, n1_ref, dproj_sc, gains_ref, parts, n1_sc, gain_sc)


def proj_parts(fsdp, first, n1_ref, dproj_ref, gains_ref, parts, n1_sc, gain_sc):
    me = lax.axis_index(FSDP)
    own = n1_ref.shape[1] // fsdp
    split_columns(gains_ref[...], gain_sc, fsdp)
    split_columns(n1_ref[...], n1_sc, fsdp)
    for i, part in enumerate(parts):
        r = first + i
        part[:own, :] = dot_tn(n1_sc[me ^ r], dproj_ref[...]).astype(LOW)
        part[own:, :own] = gain_sc[me ^ r]
        part[own:, own:] = jnp.zeros((GAIN_ROWS, dproj_ref.shape[1] - own), LOW)


def proj_rest_body(fsdp, n1_ref, dproj_ref, gains_ref, *refs):
    proj_parts(fsdp, 0, n1_ref, dproj_ref, gains_ref, refs[:-2], *refs[-2:])


def pack_body(attn_ref, mlp_ref, k_ref, v_ref, packed_ref):
    own = k_ref.shape[0]
    packed_ref[:own, :] = jnp.concatenate([k_ref[...], v_ref[...]], 1)
    gains = jnp.concatenate(
        [
            attn_ref[...].astype(F32).reshape(1, own),
            mlp_ref[...].astype(F32).reshape(1, own),
            jnp.zeros((GAIN_ROWS - 2, own), F32),
        ],
        0,
    ).astype(LOW)
    packed_ref[own:, :own] = gains
    packed_ref[own:, own:] = jnp.zeros((GAIN_ROWS, packed_ref.shape[1] - own), LOW)


def swap(values, axis, size, bit):
    return lax.ppermute(values, axis, [(i, i ^ (1 << bit)) for i in range(size)])


def bits_of(size):
    return size.bit_length() - 1


def gather(shard, size, relay=None):
    held = [(0, shard)]
    for bit in reversed(range(bits_of(size))):
        if relay is not None and bit == bits_of(size) - 1 and bit > 0:
            held.append((1 << bit, relayed(shard, size, bit, *relay)))
        else:
            held += [(r ^ (1 << bit), swap(block, FSDP, size, bit)) for r, block in held]
    return [r for r, _ in held], [block for _, block in held]


def pick_body(axis, bit, whole_ref, half_ref):
    mine = (lax.axis_index(REP) >> bit) & 1
    half_ref[...] = whole_ref[half_at(axis, half_ref.shape[axis], mine)]


def relayed(shard, size, bit, rep, rep_bit, axis):
    shape = list(shard.shape)
    shape[axis] //= 2
    (sent,) = small(functools.partial(pick_body, axis, rep_bit), [(tuple(shape), LOW)], shard)
    direct = swap(sent, FSDP, size, bit)
    other = swap(direct, REP, rep, rep_bit)
    (block,) = small(
        functools.partial(join_body, axis, rep_bit),
        [(shard.shape, LOW)],
        direct, other,
    )
    return block


def small(body, outs, *operands):
    return pl.pallas_call(
        body,
        out_shape=[jax.ShapeDtypeStruct(shape, kind) for shape, kind in outs],
        in_specs=[VMEM] * len(operands),
        out_specs=[VMEM] * len(outs),
        compiler_params=pltpu.CompilerParams(vmem_limit_bytes=SMALL_BYTES),
    )(*operands)


def half_at(axis, half, index):
    at = pl.ds(pl.multiple_of(index * half, half), half)
    return (at, slice(None)) if axis == 0 else (slice(None), at)


def add_body(count, *refs):
    total = refs[0][...].astype(F32)
    for ref in refs[1:count]:
        total = total + ref[...].astype(F32)
    refs[count][...] = total.astype(refs[count].dtype)


def add_split_body(count, axis, bit, *refs):
    sent_ref, kept_ref = refs[count:]
    mine = (lax.axis_index(REP) >> bit) & 1
    half = kept_ref.shape[axis]
    for target, index in ((sent_ref, 1 - mine), (kept_ref, mine)):
        at = half_at(axis, half, index)
        total = refs[0][at].astype(F32)
        for ref in refs[1:count]:
            total = total + ref[at].astype(F32)
        target[...] = total.astype(LOW)


def join_body(axis, bit, own_ref, other_ref, joined_ref):
    mine = (lax.axis_index(REP) >> bit) & 1
    half = own_ref.shape[axis]
    joined_ref[half_at(axis, half, mine)] = own_ref[...].astype(joined_ref.dtype)
    joined_ref[half_at(axis, half, 1 - mine)] = other_ref[...].astype(joined_ref.dtype)


def join_proj_body(own, qw, kw, own_ref, other_ref, q_ref, k_ref, v_ref, attn_ref, mlp_ref, joined):
    mine = lax.axis_index(REP) & 1
    half = own_ref.shape[0]
    joined[half_at(0, half, mine)] = own_ref[...].astype(F32)
    joined[half_at(0, half, 1 - mine)] = other_ref[...].astype(F32)
    q_ref[...] = joined[:own, :qw]
    k_ref[...] = joined[:own, qw : qw + kw]
    v_ref[...] = joined[:own, qw + kw :]
    attn_ref[...] = joined[own : own + 1, :own].reshape(own)
    mlp_ref[...] = joined[own + 1 : own + 2, :own].reshape(own)


def scatter_terms(parts, size):
    for bit in range(bits_of(size)):
        terms = []
        for i in range(0, len(parts), 2):
            arrived = swap(parts[i + 1], FSDP, size, bit)
            if len(parts) > 2 and i % 4 == 2:
                (arrived,) = small(
                    functools.partial(add_body, 2),
                    [(arrived.shape, LOW)],
                    parts[i], arrived,
                )
                terms.append(arrived)
            else:
                terms.append((parts[i], arrived))
        if len(terms) == 1:
            return flat(terms[0])
        parts = terms
    return flat(parts[0])


def flat(term):
    return sum((flat(t) for t in term), []) if isinstance(term, tuple) else [term]


def total_over(terms, size, halvings, axis):
    shape = list(terms[0].shape)
    for bit in range(bits_of(size)):
        if bit < halvings:
            shape[axis] //= 2
            sent, kept = small(
                functools.partial(add_split_body, len(terms), axis, bit),
                [(tuple(shape), LOW)] * 2,
                *terms,
            )
            terms = [kept, swap(sent, REP, size, bit)]
        else:
            (total,) = small(functools.partial(add_body, len(terms)), [(tuple(shape), LOW)], *terms)
            terms = [total, swap(total, REP, size, bit)]
    (total,) = small(
        functools.partial(add_body, len(terms)),
        [(tuple(shape), F32 if halvings == 0 else LOW)],
        *terms,
    )
    for bit in reversed(range(1, halvings)):
        shape[axis] *= 2
        (total,) = small(
            functools.partial(join_body, axis, bit),
            [(tuple(shape), LOW)],
            total, swap(total, REP, size, bit),
        )
    return total


def join_crop_body(bit, own_ref, other_ref, cropped_ref, joined):
    mine = (lax.axis_index(REP) >> bit) & 1
    half = own_ref.shape[0]
    joined[half_at(0, half, mine)] = own_ref[...].astype(joined.dtype)
    joined[half_at(0, half, 1 - mine)] = other_ref[...].astype(joined.dtype)
    cropped_ref[...] = joined[: cropped_ref.shape[0], :]


def restored(shard, size, axis, crop=None):
    shape = list(shard.shape)
    shape[axis] *= 2
    if crop is not None:
        run = pl.pallas_call(
            functools.partial(join_crop_body, 0),
            name="j",
            out_shape=jax.ShapeDtypeStruct((crop, shape[1]), F32),
            in_specs=[VMEM, VMEM],
            out_specs=VMEM,
            scratch_shapes=[pltpu.VMEM(tuple(shape), F32)],
            compiler_params=pltpu.CompilerParams(vmem_limit_bytes=SMALL_BYTES),
        )
        return run(shard, swap(shard, REP, size, 0))
    return small(
        functools.partial(join_body, axis, 0),
        [(tuple(shape), F32)],
        shard, swap(shard, REP, size, 0),
    )[0]


def shards(
    fsdp,
    rep,
    block_input,
    query_weight,
    key_weight,
    value_weight,
    out_weight,
    gate_weight,
    up_weight,
    down_weight,
    attn_gain,
    mlp_gain,
    segment_ids,
    doc_positions,
    out_cotangent,
):
    num_seqs, rows, width = block_input.shape
    assert num_seqs == 1
    keys = segment_ids.shape[1]
    own = width // fsdp
    qw, kw, ff = query_weight.shape[1], key_weight.shape[1], gate_weight.shape[1]
    pw = qw + 2 * kw
    half = fsdp // 2
    xt = block_input[0].T
    dyt = out_cotangent[0].T
    seg = segment_ids
    down_t = down_weight.T

    packed = pl.pallas_call(
        pack_body,
        name="p",
        out_shape=jax.ShapeDtypeStruct((own + GAIN_ROWS, 2 * kw), LOW),
        in_specs=[VMEM] * 4,
        out_specs=VMEM,
        compiler_params=pltpu.CompilerParams(vmem_limit_bytes=60 << 20),
    )(attn_gain, mlp_gain, key_weight, value_weight)
    rel, wkv = gather(packed, fsdp)
    _, wq = gather(query_weight, fsdp)

    scaled, cosines, sines, packed_here = call(
        prepare_body,
        [((rows, width), F32), ((rows, 128), F32), ((rows, 128), F32), (packed.shape, LOW)],
        [],
        100 * rows * width,
        8 * rows * width,
        xt, doc_positions, packed,
    )
    wkv = [packed_here] + wkv[1:]

    n1, kv_own, gains = call(
        functools.partial(project_kv_body, fsdp, rel),
        [((rows, width), LOW), ((rows, 2 * kw), LOW), ((GAIN_ROWS, width), F32)],
        [((fsdp, GAIN_ROWS, own), F32), ((fsdp, rows, own), LOW), ((rows, 2 * kw), F32)],
        2 * rows * width * 2 * kw,
        4 * width * pw,
        scaled, cosines, sines, *wkv,
    )
    (q,) = call(
        functools.partial(project_q_body, fsdp, rel),
        [((rows, qw), LOW)],
        [((fsdp, rows, own), LOW), ((rows, -(-qw // 128) * 128), F32)],
        2 * rows * width * qw,
        4 * width * qw,
        n1, cosines, sines, *wq,
    )
    _, kv = gather(kv_own, fsdp)
    many = rep > 1
    _, outs = gather(out_weight, fsdp)
    _, gates = gather(gate_weight, fsdp, (rep, 0, 1) if many else None)
    _, ups = gather(up_weight, fsdp, (rep, min(1, bits_of(rep) - 1), 1) if many else None)
    _, downs = gather(down_t, fsdp)

    def head_scratch(count):
        return [((count * GROUP, rows, HD), LOW), ((count, keys, HD), LOW), ((count, keys, HD), LOW)]

    ctxs, lses, limit = [], [], None
    for kh in range(KVH):
        ctx, lse, *made = call(
            functools.partial(attend_body, fsdp, rel, kh),
            [((rows, GROUP * HD), LOW), ((GROUP, 8, rows), F32)]
            + [((keys, rows), F32)] * (kh == 0),
            head_scratch(1) + [((GROUP * HD, rows), F32)],
            4 * GROUP * HD * rows * keys * 4,
            4 * keys * rows,
            q, seg if kh == 0 else limit, *kv,
        )
        ctxs.append(ctx)
        lses.append(lse)
        limit = made[0] if kh == 0 else limit
    h1, n2, gp, up, act, *down_late = call(
        functools.partial(feed_body, fsdp, rel),
        [((rows, width), F32), ((rows, width), LOW),
         ((rows, ff), F32), ((rows, ff), F32), ((rows, ff), LOW)]
        + [((width, ff // fsdp), LOW)] * half,
        [((fsdp, rows, own), LOW), ((fsdp, rows, qw // fsdp), LOW)],
        6 * rows * width * ff,
        12 * width * ff,
        xt, gains, dyt, *ctxs, *gates, *ups, *outs,
    )
    down_early = call(
        functools.partial(down_rest_body, fsdp),
        [((width, ff // fsdp), LOW)] * half,
        [],
        rows * width * ff,
        2 * width * ff,
        dyt, act,
    )
    yt, dgu, *gate_late = call(
        functools.partial(feed_back_body, fsdp, rel),
        [((width, rows), LOW), ((rows, 2 * ff), LOW)] + [((own, ff), LOW)] * half,
        [((fsdp, rows, own), LOW)],
        8 * rows * width * ff,
        12 * width * ff,
        gp, up, act, dyt, h1, n2, *downs,
    )
    gate_up_rest = call(
        functools.partial(gate_up_rest_body, fsdp),
        [((own, ff), LOW)] * (3 * half),
        [((fsdp, rows, own), LOW)],
        3 * rows * width * ff,
        4 * width * ff,
        n2, dgu,
    )
    up_late, gate_early, up_early = (
        gate_up_rest[i * half : (i + 1) * half] for i in range(3)
    )
    dh1, dctx, mlp_gain_grad, *out_parts = call(
        functools.partial(stream_back_body, fsdp, rel),
        [((rows, width), F32), ((rows, qw), LOW), ((8, width), F32)]
        + [((-(-qw // fsdp // 32) * 32, width), LOW)] * fsdp,
        [((fsdp, rows, own), F32), ((fsdp, rows, qw // fsdp), LOW), ((fsdp, rows, qw // fsdp), F32)],
        4 * rows * width * ff,
        8 * width * ff,
        dgu, dyt, h1, gains, *ctxs, *gates, *ups, *outs,
    )
    dqps, kv_parts, earlier = [], [], []
    for kh in range(KVH):
        last = kh == KVH - 1
        dqp, *kv_parts = call(
            functools.partial(attend_back_body, fsdp, rel, kh),
            [((rows, GROUP * HD), LOW)] + [((rows, 2 * (kw if last else HD)), LOW)] * fsdp,
            head_scratch(1) + [((GROUP, rows, HD), LOW), ((GROUP * HD + HD, rows), F32),
                               ((keys, HD), F32), ((keys, HD), F32)],
            10 * GROUP * HD * rows * keys * 4,
            4 * keys * rows,
            q, limit, lses[kh], dctx, cosines, sines, *kv, *(earlier if last else ()),
        )
        dqps.append(dqp)
        earlier += kv_parts
    dkv_terms = scatter_terms(kv_parts, fsdp)
    (dkv,) = small(functools.partial(add_body, len(dkv_terms)), [((rows, 2 * kw), LOW)], *dkv_terms)
    dxt, dproj, gain_grads, *proj_late = call(
        functools.partial(project_back_body, fsdp, rel),
        [((width, rows), LOW), ((rows, pw), LOW), ((GAIN_ROWS, width), LOW)]
        + [((own + GAIN_ROWS, pw), LOW)] * half,
        [((fsdp, rows, own), LOW), ((fsdp, rows, own), F32),
         ((fsdp, GAIN_ROWS, own), LOW)],
        4 * rows * width * pw,
        8 * width * pw,
        xt, n1, dkv, dh1, cosines, sines, gains, mlp_gain_grad, *dqps, *wq, *wkv,
    )

    proj_early = call(
        functools.partial(proj_rest_body, fsdp),
        [((own + GAIN_ROWS, pw), LOW)] * half,
        [((fsdp, rows, own), LOW), ((fsdp, GAIN_ROWS, own), LOW)],
        rows * width * pw,
        4 * width * pw,
        n1, dproj, gain_grads,
    )

    def reduced(parts, halvings, axis):
        terms = scatter_terms(parts, fsdp)
        return total_over(terms, rep, min(halvings, bits_of(rep)), axis)

    down_shard = reduced([*down_early, *down_late], 1, 0)
    down_total = restored(down_shard, rep, 0)
    gate_shard = reduced([*gate_early, *gate_late], 2, 1)
    gate_total = restored(gate_shard, rep, 1)
    up_shard = reduced([*up_early, *up_late], 2, 1)
    up_total = restored(up_shard, rep, 1)
    out_shard = reduced(out_parts, 1, 0)
    out_total = restored(out_shard, rep, 0, qw // fsdp)
    proj_shard = reduced([*proj_early, *proj_late], 1, 0)
    other = swap(proj_shard, REP, rep, 0)
    run = pl.pallas_call(
        functools.partial(join_proj_body, own, qw, kw),
        name="j",
        out_shape=[
            jax.ShapeDtypeStruct(shape, F32)
            for shape in ((own, qw), (own, kw), (own, kw), (own,), (own,))
        ],
        in_specs=[VMEM, VMEM],
        out_specs=[VMEM] * 5,
        scratch_shapes=[pltpu.VMEM((own + GAIN_ROWS, pw), F32)],
        compiler_params=pltpu.CompilerParams(vmem_limit_bytes=SMALL_BYTES),
    )
    grad_q, grad_k, grad_v, grad_attn_gain, grad_mlp_gain = run(proj_shard, other)
    return (
        yt.T[None],
        dxt.T[None],
        grad_q,
        grad_k,
        grad_v,
        out_total,
        gate_total,
        up_total,
        down_total.T,
        grad_attn_gain,
        grad_mlp_gain,
    )


def solution(mesh):
    in_specs = (
        P(REP, FSDP, None),
        P(FSDP, None),
        P(FSDP, None),
        P(FSDP, None),
        P(FSDP, None),
        P(FSDP, None),
        P(FSDP, None),
        P(FSDP, None),
        P(FSDP),
        P(FSDP),
        P(REP, None),
        P(REP, FSDP),
        P(REP, FSDP, None),
    )
    out_specs = (
        P(REP, FSDP, None),
        P(REP, FSDP, None),
        P(FSDP, None),
        P(FSDP, None),
        P(FSDP, None),
        P(FSDP, None),
        P(FSDP, None),
        P(FSDP, None),
        P(FSDP, None),
        P(FSDP),
        P(FSDP),
    )

    def body(*arrays):
        return shards(mesh.shape[FSDP], mesh.shape[REP], *arrays)

    return jax.shard_map(body, mesh=mesh, in_specs=in_specs, out_specs=out_specs, check_vma=False)
```
